512 devices in a mesh: lat: 16 (over y, core), lon: 32 (over x, z).
Axes of the slice: x: 4, y: 8, z: 8, core: 2. Of those that a mesh axis runs over, the one named last changes fastest.
Arguments:
- background_expectation: float32 [3, 128, 4096], P(None, 'lat', 'lon'), may hold values from -6 to 6
- factor: float32 [32, 3, 128, 4096], P(None, None, 'lat', 'lon'), may hold values from -6 to 6
- average_thickness: float32 [128, 4096], P('lat', 'lon'), may hold values from 1 to 2
- obs_cells: int32 [131072], P(('lat', 'lon')), may hold values from 0 to 1023
- obs_count: int32 [512], P(('lat', 'lon')), may hold values from 64 to 256, as said below
- obs_values: float32 [131072], P(('lat', 'lon')), may hold values from -384 to 384
- obs_error: float32 [131072], P(('lat', 'lon')), may hold values from 20 to 200
Outputs:
- updated_expectation: float32 [3, 128, 4096], P(None, 'lat', 'lon')
- analysis_factor: float32 [32, 3, 128, 4096], P(None, None, 'lat', 'lon')
The draws below stay inside these ranges and needn't reach their ends.
Inputs may be any that keep to these rules, and one draw needn't show every extreme that they name: `obs_cells`: each entry is a cell of the block of the device that holds the slot, row-major over its 8 x 128 cells. Device d uses its first obs_count[d] slots; some device uses all 256.
All inputs are finite; a program needn't handle non-finite values.
Results may differ from the reference program's by a relative error of at most 0.00027.
Values sent between devices are 32-bit elements; how exact they have to be, the bound alone decides.
No kernel may reach another device: no remote copies, remote signals or barrier semaphores. Data moves between devices by JAX's collectives and lax.ppermute only.
A program may use at most 64 MiB of HBM per device.

```python
import math
import jax
import jax.numpy as jnp
from jax import lax

SPREAD_RANK = 32
STEPS = 4
LAT_DEV = 8
LON_DEV = 128
OBS_DEV = 256
MERIDIAN_CELLS = 128
PARALLEL_CELLS = 4096
NOBS = 131072
N_LON = 32
DEVICES = 512


def draw_obs_count(key, part):
    first_key, second_key = jax.random.split(jax.random.fold_in(key, 17))
    counts = jax.random.randint(first_key, (DEVICES,), OBS_DEV // 4, OBS_DEV + 1)
    chosen = jax.random.randint(second_key, (), 0, DEVICES)
    return jnp.where(jnp.arange(DEVICES) == chosen, OBS_DEV, counts).astype(jnp.int32)


def set_ends(drawn, rng, low, largest):
    dims = drawn.shape
    spot = [jax.random.randint(jax.random.fold_in(rng, axis), (), 0, dims[axis]) for axis in range(len(dims))]
    drawn = drawn.at[tuple(spot)].set(low)
    longest = dims.index(max(dims))
    spot[longest] = (spot[longest] + 1) % dims[longest]
    return drawn.at[tuple(spot)].set(largest)


def shard_levels(own_key, extent, shards, low, top_value):
    loudness, own = 1.0, jax.random.fold_in(own_key, 6)
    for axis_at, blocks in shards:
        heights = jnp.exp(jax.random.uniform(jax.random.fold_in(own, axis_at), (blocks,), jnp.float32, low / len(shards), top_value / len(shards)))
        loudness = loudness * jnp.repeat(heights, extent[axis_at] // blocks).reshape([-1 if axis == axis_at else 1 for axis in range(len(extent))])
    return loudness


def gaussian(rng, dims, deviation, reach, pieces=(), held_as=jnp.bfloat16):
    entries = jax.random.normal(rng, dims, jnp.float32) * deviation
    if len(pieces) > 0:
        entries = shard_levels(rng, dims, pieces, -0.22, 0.18) * entries
    return jnp.clip(entries, min=-reach, max=reach).astype(held_as)


def setup_inputs(seed: int = 0) -> dict:
    streams_of = jax.random.split(jax.random.key(seed), 8)
    return {
        "background_expectation": gaussian(streams_of[0], (3, MERIDIAN_CELLS, PARALLEL_CELLS), 1.0, 6.0, ((1, 16), (2, 32)), jnp.float32),
        "factor": gaussian(streams_of[1], (SPREAD_RANK, 3, MERIDIAN_CELLS, PARALLEL_CELLS), 1.0, 6.0, ((2, 16), (3, 32)), jnp.float32),
        "average_thickness": jnp.clip(jnp.exp(math.log(2.0) - 0.6931472 * jax.random.uniform(streams_of[2], (MERIDIAN_CELLS, PARALLEL_CELLS), jnp.float32) ** shard_levels(streams_of[2], (MERIDIAN_CELLS, PARALLEL_CELLS), ((0, 16), (1, 32)), -0.2, 0.2)), 1.0, 2.0),
        "obs_cells": set_ends(jax.random.randint(streams_of[3], (NOBS,), 0, LAT_DEV * LON_DEV), jax.random.fold_in(streams_of[3], 1), 0, (LAT_DEV * LON_DEV) - 1).astype(jnp.int32),
        "obs_count": draw_obs_count(jax.random.fold_in(streams_of[7], 71), 0),
        "obs_values": gaussian(streams_of[5], (NOBS,), 60.0, 384.0, ((0, 512),), jnp.float32),
        "obs_error": jnp.clip(jnp.exp(math.log(200.0) - 2.3025851 * jax.random.uniform(streams_of[6], (NOBS,), jnp.float32) ** shard_levels(streams_of[6], (NOBS,), ((0, 512),), -0.2, 0.2)), 20.0, 200.0),
    }


TIME_STEP = 0.9
ROTATION = 0.25

def lon_diff(field):
    return 0.5 * (jnp.roll(field, -1, 1) - jnp.roll(field, 1, 1))

def lat_diff(field):
    padded = jnp.pad(field, ((1, 1), (0, 0)))
    return 0.5 * (padded[2:] - padded[:-2])

def advanced_spread_vector(spread_vector, average_thickness):
    height, east_wind, north_wind = (spread_vector[0], spread_vector[1], spread_vector[2])
    for repeat in range(STEPS):
        divergence = lon_diff(east_wind) + lat_diff(north_wind)
        height = height - TIME_STEP * average_thickness * divergence
        new_east = east_wind - TIME_STEP * lon_diff(height) + ROTATION * north_wind
        north_wind = north_wind - TIME_STEP * lat_diff(height) - ROTATION * east_wind
        east_wind = new_east
    return jnp.stack([height, east_wind, north_wind], 0)

def reference(background_expectation, factor, average_thickness, obs_cells, obs_count, obs_values, obs_error):
    joined_components = jnp.concatenate([background_expectation[None], factor], 0)
    propagated_spread = lax.map(lambda spread_vector: advanced_spread_vector(spread_vector, average_thickness), joined_components)
    position = jnp.arange(NOBS, dtype=jnp.int32)
    device = position // OBS_DEV
    band = device // N_LON
    cycle = device % N_LON
    row_index = band * LAT_DEV + obs_cells // LON_DEV
    col_index = cycle * LON_DEV + obs_cells % LON_DEV
    global_cell = (row_index * PARALLEL_CELLS + col_index).astype(jnp.int32)
    live = (position % OBS_DEV < obs_count[device]).astype(jnp.float32)
    weight = live / obs_error
    surface_elevation = propagated_spread[:, 0].reshape(SPREAD_RANK + 1, MERIDIAN_CELLS * PARALLEL_CELLS)
    picked = jnp.take(surface_elevation, global_cell, axis=1)
    scaled = picked[1:] * weight
    innovation = (obs_values - picked[0]) * weight
    gram = jnp.dot(scaled, scaled.T, precision=lax.Precision.HIGHEST)
    drive = jnp.dot(scaled, innovation, precision=lax.Precision.HIGHEST)
    identity = jnp.eye(SPREAD_RANK, dtype=jnp.float32)
    system = identity + gram
    lower = jnp.linalg.cholesky(system)
    inverse = lax.linalg.triangular_solve(lower, identity, left_side=True, lower=True, transpose_a=True)
    middle = lax.linalg.triangular_solve(lower, drive[:, None], left_side=True, lower=True)
    difference_coefficients = lax.linalg.triangular_solve(lower, middle, left_side=True, lower=True, transpose_a=True)[:, 0]
    sample_realisations = propagated_spread[1:].reshape(SPREAD_RANK, -1)
    analysis_factor = jnp.dot(inverse.T, sample_realisations, precision=lax.Precision.HIGHEST).reshape(factor.shape)
    updated_expectation = propagated_spread[0] + jnp.dot(difference_coefficients, sample_realisations, precision=lax.Precision.HIGHEST).reshape(background_expectation.shape)
    return (updated_expectation, analysis_factor)
```

```python
import functools

import jax
import jax.numpy as jnp
from jax import lax
from jax.experimental import pallas as pl
from jax.experimental.pallas import tpu as pltpu
from jax.sharding import PartitionSpec as P

STEPS = 4
TIME_STEP = 0.9
ROTATION = 0.25

RANK = 32
ROWS = 8
LANES = 128
HALO = 2 * STEPS
TILES = RANK // 8
PLANES = 3 * ROWS
PACK = 3 * RANK + 8
HIGHEST = lax.Precision.HIGHEST
NT = (((1,), (1,)), ((), ()))


def lane_iota():
    return lax.broadcasted_iota(jnp.int32, (8, LANES), 1)


def member_rows(field, row, tile):
    return pl.ds(8 * tile * PLANES + field * ROWS + row, 8, stride=PLANES)


def small_tile(mean_ref, depth_ref, row):
    return jnp.concatenate(
        [mean_ref[f * ROWS + row : f * ROWS + row + 1, :] for f in range(3)]
        + [depth_ref[row : row + 1, :]] * 5,
        0,
    )


def pack_kernel(factor_ref, mean_ref, depth_ref, out_ref):
    group = lane_iota() // 16

    def packed(row_value):
        acc = None
        for row in range(ROWS):
            moved = pltpu.roll(row_value(row), (HALO + 16 * row) % LANES, 1)
            acc = moved if acc is None else jnp.where(group == row, moved, acc)
        return acc

    for field in range(3):
        for tile in range(TILES):
            out_ref[field * RANK + 8 * tile : field * RANK + 8 * tile + 8, :] = packed(
                lambda row: factor_ref[member_rows(field, row, tile), :]
            )
    out_ref[3 * RANK : PACK, :] = packed(lambda row: small_tile(mean_ref, depth_ref, row))


def obs_kernel(count_ref, cells_ref, values_ref, error_ref, out_ref):
    slots = cells_ref.shape[1]
    live = lax.broadcasted_iota(jnp.int32, (1, slots), 1) < count_ref[0]
    weight = jnp.where(live, 1.0, 0.0) / error_ref[...]
    square = weight * weight
    cells = cells_ref[...]
    row_of = cells // LANES
    lane_of = cells - row_of * LANES
    in_row = lax.broadcasted_iota(jnp.int32, (ROWS, slots), 0) == row_of
    spread = jnp.concatenate(
        [jnp.where(in_row, square, 0.0), jnp.where(in_row, square * values_ref[...], 0.0)], 0
    )
    in_lane = lax.broadcasted_iota(jnp.int32, (LANES, slots), 0) == lane_of
    out_ref[...] = lax.dot_general(
        spread, jnp.where(in_lane, 1.0, 0.0), NT, precision=HIGHEST, preferred_element_type=jnp.float32
    )


def forecast_kernel(
    own_ref, north_ref, south_ref, mean_ref, depth_ref, edge_ref, north_edge_ref, south_edge_ref,
    weight_ref, split_ref, mean_out_ref, gram_ref, state, depth, heights, scaled,
):
    lane = lane_iota()
    left, right = lane >= LANES - HALO, lane < HALO
    band = lax.axis_index("lat")
    bands = lax.axis_size("lat")

    def windows(value, edge, row):
        moved = pltpu.roll(edge, (LANES - HALO - 16 * row) % LANES, 1)
        return jnp.where(left, moved, value), jnp.where(right, moved, value)

    blocks = (
        (north_ref, north_edge_ref, lambda r: north_edge_ref[PACK + 8 * r : PACK + 8 * r + 8, :]),
        (own_ref, edge_ref, lambda r: small_tile(mean_ref, depth_ref, r)),
        (south_ref, south_edge_ref, lambda r: south_edge_ref[PACK + 8 * r : PACK + 8 * r + 8, :]),
    )
    for block, (main, edges, small) in enumerate(blocks):
        for field in range(3):
            for tile in range(TILES):
                edge = edges[field * RANK + 8 * tile : field * RANK + 8 * tile + 8, :]
                for row in range(ROWS):
                    west, east = windows(main[member_rows(field, row, tile), :], edge, row)
                    state[2 * tile, field, ROWS * block + row] = west
                    state[2 * tile + 1, field, ROWS * block + row] = east
        edge = edges[3 * RANK : PACK, :]
        for row in range(ROWS):
            at = ROWS * block + row
            west, east = windows(small(row), edge, row)
            for field in range(3):
                state[2 * TILES, field, at, 0:1, :] = west[field : field + 1, :]
                state[2 * TILES, field, at, 1:2, :] = east[field : field + 1, :]
                state[2 * TILES, field, at, 2:8, :] = west[2:8, :]
            scaled_west = (0.5 * TIME_STEP) * west[3:4, :]
            scaled_east = (0.5 * TIME_STEP) * east[3:4, :]
            depth[0, at] = jnp.broadcast_to(scaled_west, (8, LANES))
            depth[1, at] = jnp.broadcast_to(scaled_east, (8, LANES))
            depth[2, at] = jnp.where(
                lax.broadcasted_iota(jnp.int32, (8, LANES), 0) == 0, depth[0, at], depth[1, at]
            )

    pull = 0.5 * TIME_STEP
    north_pull = jnp.where(band > 0, pull, 0.0)
    south_pull = jnp.where(band < bands - 1, pull, 0.0)

    def lon_difference(value):
        return pltpu.roll(value, LANES - 1, 1) - pltpu.roll(value, 1, 1)

    def advance(which, carry):
        plane = jnp.where(which == 2 * TILES, 2, which & 1)
        h, e, n = (state.at[which, field] for field in range(3))
        for step in range(STEPS):
            first, last = 1 + 2 * step, 3 * ROWS - 2 - 2 * step
            for row in range(first, last + 1):
                divergence = lon_difference(e[row]) + (n[row + 1] - n[row - 1])
                h[row] = h[row] - depth[plane, row] * divergence
            for row in range(first + 1, last):
                row_pull = north_pull if row < ROWS else south_pull if row >= 2 * ROWS else pull
                east, north = e[row], n[row]
                e[row] = east - pull * lon_difference(h[row]) + ROTATION * north
                n[row] = north - row_pull * (h[row + 1] - h[row - 1]) - ROTATION * east
        return carry

    lax.fori_loop(0, 2 * TILES + 1, advance, 0)

    half = lane < LANES // 2
    half_row = lax.broadcasted_iota(jnp.int32, (1, LANES), 1) < LANES // 2
    for field in range(3):
        for row in range(ROWS):
            cols = slice((field * ROWS + row) * LANES, (field * ROWS + row + 1) * LANES)
            full = jnp.concatenate(
                [
                    jnp.where(half, state[2 * t, field, ROWS + row], state[2 * t + 1, field, ROWS + row])
                    for t in range(TILES)
                ],
                0,
            )
            high = full.astype(jnp.bfloat16)
            rest = full - high.astype(jnp.float32)
            middle = rest.astype(jnp.bfloat16)
            split_ref[0:RANK, cols] = high
            split_ref[RANK : 2 * RANK, cols] = middle
            split_ref[2 * RANK : 3 * RANK, cols] = (rest - middle.astype(jnp.float32)).astype(jnp.bfloat16)
            both = state[2 * TILES, field, ROWS + row]
            mean = jnp.where(half_row, both[0:1, :], both[1:2, :])
            mean_out_ref[field * ROWS + row : field * ROWS + row + 1, :] = mean
            if field == 0:
                square = weight_ref[row : row + 1, :]
                heights[:, cols] = full
                scaled[0:RANK, cols] = full * square
                pulled = weight_ref[ROWS + row : ROWS + row + 1, :] - square * mean
                scaled[RANK : RANK + 8, cols] = jnp.broadcast_to(pulled, (8, LANES))
    gram = lax.dot_general(
        heights[...], scaled[...], NT, precision=HIGHEST, preferred_element_type=jnp.float32
    )
    gram = jnp.concatenate([gram, jnp.zeros((RANK, LANES - RANK - 8), jnp.float32)], 1)
    acc = None
    for tile in range(TILES):
        part = gram[8 * tile : 8 * tile + 8, :]
        if tile < 2:
            far = gram[8 * tile + 16 : 8 * tile + 24, :]
            part = jnp.where(lane == 31, pltpu.roll(part, LANES - 1, 1), part)
            part = jnp.where(lane == 30, pltpu.roll(far, LANES - 2, 1), part)
        moved = pltpu.roll(part, 32 * tile, 1) if tile else part
        acc = moved if acc is None else jnp.where(lane // 32 == tile, moved, acc)
    gram_ref[...] = acc


def analysis_kernel(parts_ref, split_ref, mean_ref, update_ref, factor_ref):
    lane = lane_iota()
    total = jnp.sum(parts_ref[...], 0)
    tiles, drives = [], [None] * TILES
    for tile in range(TILES):
        part = pltpu.roll(total, LANES - 32 * tile, 1) if tile else total
        if tile < 2:
            drives[tile] = pltpu.roll(part, 2 * RANK - 31, 1)
            drives[tile + 2] = pltpu.roll(part, 2 * RANK - 30, 1)
        tiles.append(part)
    lower = jnp.concatenate(tiles, 0)
    wide = lax.broadcasted_iota(jnp.int32, (RANK, LANES), 1)
    deep = lax.broadcasted_iota(jnp.int32, (RANK, LANES), 0)
    mirrored = jnp.concatenate([lower, jnp.zeros((LANES - RANK, LANES), jnp.float32)], 0).T[0:RANK, :]
    work = jnp.where(wide > deep, mirrored, lower)
    work = jnp.where(wide < RANK, work, 0.0) + jnp.where((wide == deep) | (wide == deep + RANK), 1.0, 0.0)
    work = jnp.where(wide == 2 * RANK, jnp.concatenate(drives, 0), work)
    for k in range(RANK - 1):
        row = work[k : k + 1, :] * (1.0 / work[k : k + 1, k : k + 1])
        column = jnp.where(deep[:, 0:1] > k, work[:, k : k + 1], 0.0)
        work = work - column * row
    pivots = jnp.sum(jnp.where(wide == deep, work, 0.0), 1, keepdims=True)
    work = work * lax.rsqrt(pivots)
    shift = jnp.sum(work * work[:, 2 * RANK : 2 * RANK + 1], 0, keepdims=True)
    mixed = jnp.concatenate([work, jnp.broadcast_to(shift, (8, LANES))], 0)[:, RANK : 2 * RANK]
    high = mixed.astype(jnp.bfloat16)
    rest = mixed - high.astype(jnp.float32)
    middle = rest.astype(jnp.bfloat16)
    low = (rest - middle.astype(jnp.float32)).astype(jnp.bfloat16)
    left = jnp.concatenate([high, high, high, middle, middle, low], 1)
    split = split_ref[...]
    fine = jnp.concatenate([split, split[0 : 2 * RANK], split[0:RANK]], 0)
    out = jnp.dot(left, fine, preferred_element_type=jnp.float32)
    for plane in range(PLANES):
        cols = slice(plane * LANES, (plane + 1) * LANES)
        for tile in range(TILES):
            factor_ref[pl.ds(8 * tile * PLANES + plane, 8, stride=PLANES), :] = out[8 * tile : 8 * tile + 8, cols]
        update_ref[plane : plane + 1, :] = mean_ref[plane : plane + 1, :] + out[RANK : RANK + 1, cols]


VMEM = pl.BlockSpec(memory_space=pltpu.VMEM)
SMEM = pl.BlockSpec(memory_space=pltpu.SMEM)


def f32(*shape):
    return jax.ShapeDtypeStruct(shape, jnp.float32)


def shift_by(value, axis, step, periodic):
    count = lax.axis_size(axis)
    pairs = [(i, (i + step) % count) for i in range(count) if periodic or 0 <= i + step < count]
    return lax.ppermute(value, axis, pairs)


def sum_over(value, axis):
    count = lax.axis_size(axis)
    sent = jnp.broadcast_to(value[None], (count, *value.shape))
    return lax.all_to_all(sent, axis, 0, 0)


def per_device(
    background_expectation, factor, average_thickness, obs_cells, obs_count, obs_values, obs_error
):
    assert factor.shape == (RANK, 3, ROWS, LANES)
    own = factor.reshape(RANK * PLANES, LANES)
    mean = background_expectation.reshape(PLANES, LANES)
    edges = pl.pallas_call(
        pack_kernel, out_shape=f32(PACK, LANES), in_specs=[VMEM] * 3, out_specs=VMEM, name="pack"
    )(own, mean, average_thickness)
    from_west = shift_by(edges, "lon", 1, True)
    from_east = shift_by(edges, "lon", -1, True)
    from_north = shift_by(own, "lat", 1, False)
    from_south = shift_by(own, "lat", -1, False)
    east_lane = (lax.broadcasted_iota(jnp.int32, (PACK, LANES), 1) & 8) != 0
    halo = jnp.where(east_lane, from_east, from_west)
    small = jnp.concatenate([mean.reshape(3, ROWS, LANES), average_thickness[None]], 0)
    small = jnp.concatenate([small, jnp.zeros_like(small)], 0).transpose(1, 0, 2).reshape(8 * ROWS, LANES)
    corner = jnp.concatenate([halo, small], 0)
    north_corner = shift_by(corner, "lat", 1, False)
    south_corner = shift_by(corner, "lat", -1, False)
    slots = obs_cells.shape[0]
    weights = pl.pallas_call(
        obs_kernel, out_shape=f32(2 * ROWS, LANES), in_specs=[SMEM] + [VMEM] * 3, out_specs=VMEM, name="obs"
    )(obs_count, obs_cells.reshape(1, slots), obs_values.reshape(1, slots), obs_error.reshape(1, slots))
    split, mean, gram = pl.pallas_call(
        forecast_kernel,
        out_shape=(
            jax.ShapeDtypeStruct((3 * RANK, PLANES * LANES), jnp.bfloat16),
            f32(PLANES, LANES),
            f32(8, LANES),
        ),
        in_specs=[VMEM] * 9,
        out_specs=(VMEM,) * 3,
        scratch_shapes=[
            pltpu.VMEM((2 * TILES + 1, 3, 3 * ROWS, 8, LANES), jnp.float32),
            pltpu.VMEM((3, 3 * ROWS, 8, LANES), jnp.float32),
            pltpu.VMEM((RANK, ROWS * LANES), jnp.float32),
            pltpu.VMEM((RANK + 8, ROWS * LANES), jnp.float32),
        ],
        name="forecast",
    )(own, from_north, from_south, mean, average_thickness, halo, north_corner, south_corner, weights)
    gram = jnp.sum(sum_over(gram, "lat"), 0)
    parts = sum_over(gram, "lon")
    update, analysis = pl.pallas_call(
        analysis_kernel,
        out_shape=(f32(PLANES, LANES), f32(RANK * PLANES, LANES)),
        in_specs=[VMEM] * 3,
        out_specs=(VMEM, VMEM),
        name="analysis",
    )(parts, split, mean)
    return update.reshape(background_expectation.shape), analysis.reshape(factor.shape)


def solution(mesh):
    return jax.shard_map(
        per_device,
        mesh=mesh,
        in_specs=(
            P(None, "lat", "lon"),
            P(None, None, "lat", "lon"),
            P("lat", "lon"),
            P(("lat", "lon")),
            P(("lat", "lon")),
            P(("lat", "lon")),
            P(("lat", "lon")),
        ),
        out_specs=(P(None, "lat", "lon"), P(None, None, "lat", "lon")),
        check_vma=False,
    )
```

```python
import functools

import jax
import jax.numpy as jnp
from jax import lax
from jax.experimental import pallas as pl
from jax.experimental.pallas import tpu as pltpu
from jax.sharding import PartitionSpec as P

STEPS = 4
TIME_STEP = 0.9
ROTATION = 0.25

RANK = 32
ROWS = 8
LANES = 128
HALO = 2 * STEPS
TILES = RANK // 8
PLANES = 3 * ROWS
PACK = 3 * RANK + 8
HIGHEST = lax.Precision.HIGHEST
NT = (((1,), (1,)), ((), ()))


def lane_iota():
    return lax.broadcasted_iota(jnp.int32, (8, LANES), 1)


def member_rows(field, row, tile):
    return pl.ds(8 * tile * PLANES + field * ROWS + row, 8, stride=PLANES)


def small_tile(mean_ref, depth_ref, row):
    return jnp.concatenate(
        [mean_ref[f * ROWS + row : f * ROWS + row + 1, :] for f in range(3)]
        + [depth_ref[row : row + 1, :]] * 5,
        0,
    )


def pack_kernel(factor_ref, mean_ref, depth_ref, out_ref):
    group = lane_iota() // 16

    def packed(row_value):
        acc = None
        for row in range(ROWS):
            moved = pltpu.roll(row_value(row), (HALO + 16 * row) % LANES, 1)
            acc = moved if acc is None else jnp.where(group == row, moved, acc)
        return acc

    for field in range(3):
        for tile in range(TILES):
            out_ref[field * RANK + 8 * tile : field * RANK + 8 * tile + 8, :] = packed(
                lambda row: factor_ref[member_rows(field, row, tile), :]
            )
    out_ref[3 * RANK : PACK, :] = packed(lambda row: small_tile(mean_ref, depth_ref, row))


def obs_kernel(count_ref, cells_ref, values_ref, error_ref, out_ref):
    slots = cells_ref.shape[1]
    live = lax.broadcasted_iota(jnp.int32, (1, slots), 1) < count_ref[0]
    weight = jnp.where(live, 1.0, 0.0) / error_ref[...]
    square = weight * weight
    cells = cells_ref[...]
    row_of = cells // LANES
    lane_of = cells - row_of * LANES
    in_row = lax.broadcasted_iota(jnp.int32, (ROWS, slots), 0) == row_of
    spread = jnp.concatenate(
        [jnp.where(in_row, square, 0.0), jnp.where(in_row, square * values_ref[...], 0.0)], 0
    )
    in_lane = lax.broadcasted_iota(jnp.int32, (LANES, slots), 0) == lane_of
    out_ref[...] = lax.dot_general(
        spread, jnp.where(in_lane, 1.0, 0.0), NT, precision=HIGHEST, preferred_element_type=jnp.float32
    )


def forecast_kernel(
    own_ref, north_ref, south_ref, mean_ref, depth_ref, edge_ref, north_edge_ref, south_edge_ref,
    weight_ref, split_ref, mean_out_ref, gram_ref, state, depth, heights, scaled,
):
    lane = lane_iota()
    left, right = lane >= LANES - HALO, lane < HALO
    band = lax.axis_index("lat")
    bands = lax.axis_size("lat")

    def windows(value, edge, row):
        moved = pltpu.roll(edge, (LANES - HALO - 16 * row) % LANES, 1)
        return jnp.where(left, moved, value), jnp.where(right, moved, value)

    blocks = (
        (north_ref, north_edge_ref, lambda r: north_edge_ref[PACK + 8 * r : PACK + 8 * r + 8, :]),
        (own_ref, edge_ref, lambda r: small_tile(mean_ref, depth_ref, r)),
        (south_ref, south_edge_ref, lambda r: south_edge_ref[PACK + 8 * r : PACK + 8 * r + 8, :]),
    )
    for block, (main, edges, small) in enumerate(blocks):
        for field in range(3):
            for tile in range(TILES):
                edge = edges[field * RANK + 8 * tile : field * RANK + 8 * tile + 8, :]
                for row in range(ROWS):
                    west, east = windows(main[member_rows(field, row, tile), :], edge, row)
                    state[2 * tile, field, ROWS * block + row] = west
                    state[2 * tile + 1, field, ROWS * block + row] = east
        edge = edges[3 * RANK : PACK, :]
        for row in range(ROWS):
            at = ROWS * block + row
            west, east = windows(small(row), edge, row)
            for field in range(3):
                state[2 * TILES, field, at, 0:1, :] = west[field : field + 1, :]
                state[2 * TILES, field, at, 1:2, :] = east[field : field + 1, :]
                state[2 * TILES, field, at, 2:8, :] = west[2:8, :]
            scaled_west = (0.5 * TIME_STEP) * west[3:4, :]
            scaled_east = (0.5 * TIME_STEP) * east[3:4, :]
            depth[0, at] = jnp.broadcast_to(scaled_west, (8, LANES))
            depth[1, at] = jnp.broadcast_to(scaled_east, (8, LANES))
            depth[2, at] = jnp.where(
                lax.broadcasted_iota(jnp.int32, (8, LANES), 0) == 0, depth[0, at], depth[1, at]
            )

    pull = 0.5 * TIME_STEP
    north_pull = jnp.where(band > 0, pull, 0.0)
    south_pull = jnp.where(band < bands - 1, pull, 0.0)

    def lon_difference(value):
        return pltpu.roll(value, LANES - 1, 1) - pltpu.roll(value, 1, 1)

    def advance(which, carry):
        plane = jnp.where(which == 2 * TILES, 2, which & 1)
        h, e, n = (state.at[which, field] for field in range(3))
        for step in range(STEPS):
            first, last = 1 + 2 * step, 3 * ROWS - 2 - 2 * step
            for row in range(first, last + 1):
                divergence = lon_difference(e[row]) + (n[row + 1] - n[row - 1])
                h[row] = h[row] - depth[plane, row] * divergence
            for row in range(first + 1, last):
                row_pull = north_pull if row < ROWS else south_pull if row >= 2 * ROWS else pull
                east, north = e[row], n[row]
                e[row] = east - pull * lon_difference(h[row]) + ROTATION * north
                n[row] = north - row_pull * (h[row + 1] - h[row - 1]) - ROTATION * east
        return carry

    lax.fori_loop(0, 2 * TILES + 1, advance, 0)

    half = lane < LANES // 2
    half_row = lax.broadcasted_iota(jnp.int32, (1, LANES), 1) < LANES // 2
    for field in range(3):
        for row in range(ROWS):
            cols = slice((field * ROWS + row) * LANES, (field * ROWS + row + 1) * LANES)
            full = jnp.concatenate(
                [
                    jnp.where(half, state[2 * t, field, ROWS + row], state[2 * t + 1, field, ROWS + row])
                    for t in range(TILES)
                ],
                0,
            )
            high = full.astype(jnp.bfloat16)
            rest = full - high.astype(jnp.float32)
            middle = rest.astype(jnp.bfloat16)
            split_ref[0:RANK, cols] = high
            split_ref[RANK : 2 * RANK, cols] = middle
            split_ref[2 * RANK : 3 * RANK, cols] = (rest - middle.astype(jnp.float32)).astype(jnp.bfloat16)
            both = state[2 * TILES, field, ROWS + row]
            mean = jnp.where(half_row, both[0:1, :], both[1:2, :])
            mean_out_ref[field * ROWS + row : field * ROWS + row + 1, :] = mean
            if field == 0:
                square = weight_ref[row : row + 1, :]
                heights[:, cols] = full
                scaled[0:RANK, cols] = full * square
                pulled = weight_ref[ROWS + row : ROWS + row + 1, :] - square * mean
                scaled[RANK : RANK + 8, cols] = jnp.broadcast_to(pulled, (8, LANES))
    gram = lax.dot_general(
        heights[...], scaled[...], NT, precision=HIGHEST, preferred_element_type=jnp.float32
    )
    gram = jnp.concatenate([gram, jnp.zeros((RANK, LANES - RANK - 8), jnp.float32)], 1)
    acc = None
    for tile in range(TILES):
        part = gram[8 * tile : 8 * tile + 8, :]
        if tile < 2:
            far = gram[8 * tile + 16 : 8 * tile + 24, :]
            part = jnp.where(lane == 31, pltpu.roll(part, LANES - 1, 1), part)
            part = jnp.where(lane == 30, pltpu.roll(far, LANES - 2, 1), part)
        moved = pltpu.roll(part, 32 * tile, 1) if tile else part
        acc = moved if acc is None else jnp.where(lane // 32 == tile, moved, acc)
    gram_ref[...] = acc


def analysis_kernel(parts_ref, split_ref, mean_ref, update_ref, factor_ref):
    lane = lane_iota()
    total = jnp.sum(parts_ref[...], 0)
    tiles, drives = [], [None] * TILES
    for tile in range(TILES):
        part = pltpu.roll(total, LANES - 32 * tile, 1) if tile else total
        if tile < 2:
            drives[tile] = pltpu.roll(part, 2 * RANK - 31, 1)
            drives[tile + 2] = pltpu.roll(part, 2 * RANK - 30, 1)
        tiles.append(part)
    lower = jnp.concatenate(tiles, 0)
    wide = lax.broadcasted_iota(jnp.int32, (RANK, LANES), 1)
    deep = lax.broadcasted_iota(jnp.int32, (RANK, LANES), 0)
    mirrored = jnp.concatenate([lower, jnp.zeros((LANES - RANK, LANES), jnp.float32)], 0).T[0:RANK, :]
    work = jnp.where(wide > deep, mirrored, lower)
    work = jnp.where(wide < RANK, work, 0.0) + jnp.where((wide == deep) | (wide == deep + RANK), 1.0, 0.0)
    work = jnp.where(wide == 2 * RANK, jnp.concatenate(drives, 0), work)
    for k in range(RANK - 1):
        row = work[k : k + 1, :] * (1.0 / work[k : k + 1, k : k + 1])
        column = jnp.where(deep[:, 0:1] > k, work[:, k : k + 1], 0.0)
        work = work - column * row
    pivots = jnp.sum(jnp.where(wide == deep, work, 0.0), 1, keepdims=True)
    work = work * lax.rsqrt(pivots)
    shift = jnp.sum(work * work[:, 2 * RANK : 2 * RANK + 1], 0, keepdims=True)
    mixed = jnp.concatenate([work, jnp.broadcast_to(shift, (8, LANES))], 0)[:, RANK : 2 * RANK]
    high = mixed.astype(jnp.bfloat16)
    rest = mixed - high.astype(jnp.float32)
    middle = rest.astype(jnp.bfloat16)
    low = (rest - middle.astype(jnp.float32)).astype(jnp.bfloat16)
    left = jnp.concatenate([high, high, high, middle, middle, low], 1)
    split = split_ref[...]
    fine = jnp.concatenate([split, split[0 : 2 * RANK], split[0:RANK]], 0)
    out = jnp.dot(left, fine, preferred_element_type=jnp.float32)
    for plane in range(PLANES):
        cols = slice(plane * LANES, (plane + 1) * LANES)
        for tile in range(TILES):
            factor_ref[pl.ds(8 * tile * PLANES + plane, 8, stride=PLANES), :] = out[8 * tile : 8 * tile + 8, cols]
        update_ref[plane : plane + 1, :] = mean_ref[plane : plane + 1, :] + out[RANK : RANK + 1, cols]


VMEM = pl.BlockSpec(memory_space=pltpu.VMEM)
SMEM = pl.BlockSpec(memory_space=pltpu.SMEM)


def f32(*shape):
    return jax.ShapeDtypeStruct(shape, jnp.float32)


def on_chip(value):
    return pltpu.with_memory_space_constraint(value, pltpu.VMEM)


def shift_by(value, axis, step, periodic):
    count = lax.axis_size(axis)
    pairs = [(i, (i + step) % count) for i in range(count) if periodic or 0 <= i + step < count]
    return lax.ppermute(value, axis, pairs)


def sum_over(value, axis):
    count = lax.axis_size(axis)
    sent = jnp.broadcast_to(value[None], (count, *value.shape))
    return lax.all_to_all(sent, axis, 0, 0)


def per_device(
    background_expectation, factor, average_thickness, obs_cells, obs_count, obs_values, obs_error
):
    assert factor.shape == (RANK, 3, ROWS, LANES)
    own = on_chip(factor.reshape(RANK * PLANES, LANES))
    mean = background_expectation.reshape(PLANES, LANES)
    edges = pl.pallas_call(
        pack_kernel, out_shape=pltpu.VMEM((PACK, LANES), jnp.float32), in_specs=[VMEM] * 3, out_specs=VMEM, name="pack"
    )(own, mean, average_thickness)
    from_west = shift_by(edges, "lon", 1, True)
    from_east = shift_by(edges, "lon", -1, True)
    from_north = shift_by(own, "lat", 1, False)
    from_south = shift_by(own, "lat", -1, False)
    east_lane = (lax.broadcasted_iota(jnp.int32, (PACK, LANES), 1) & 8) != 0
    halo = jnp.where(east_lane, from_east, from_west)
    small = jnp.concatenate([mean.reshape(3, ROWS, LANES), average_thickness[None]], 0)
    small = jnp.concatenate([small, jnp.zeros_like(small)], 0).transpose(1, 0, 2).reshape(8 * ROWS, LANES)
    corner = jnp.concatenate([halo, small], 0)
    north_corner = shift_by(corner, "lat", 1, False)
    south_corner = shift_by(corner, "lat", -1, False)
    slots = obs_cells.shape[0]
    weights = pl.pallas_call(
        obs_kernel, out_shape=pltpu.VMEM((2 * ROWS, LANES), jnp.float32), in_specs=[SMEM] + [VMEM] * 3, out_specs=VMEM, name="obs"
    )(obs_count, obs_cells.reshape(1, slots), obs_values.reshape(1, slots), obs_error.reshape(1, slots))
    split, mean, gram = pl.pallas_call(
        forecast_kernel,
        out_shape=(
            pltpu.VMEM((3 * RANK, PLANES * LANES), jnp.bfloat16),
            pltpu.VMEM((PLANES, LANES), jnp.float32),
            pltpu.VMEM((8, LANES), jnp.float32),
        ),
        in_specs=[VMEM] * 9,
        out_specs=(VMEM,) * 3,
        scratch_shapes=[
            pltpu.VMEM((2 * TILES + 1, 3, 3 * ROWS, 8, LANES), jnp.float32),
            pltpu.VMEM((3, 3 * ROWS, 8, LANES), jnp.float32),
            pltpu.VMEM((RANK, ROWS * LANES), jnp.float32),
            pltpu.VMEM((RANK + 8, ROWS * LANES), jnp.float32),
        ],
        name="forecast",
    )(
        own, on_chip(from_north), on_chip(from_south), mean, average_thickness,
        on_chip(halo), on_chip(north_corner), on_chip(south_corner), weights,
    )
    gram = jnp.sum(sum_over(gram, "lat"), 0)
    parts = sum_over(gram, "lon")
    update, analysis = pl.pallas_call(
        analysis_kernel,
        out_shape=(f32(PLANES, LANES), f32(RANK * PLANES, LANES)),
        in_specs=[VMEM] * 3,
        out_specs=(VMEM, VMEM),
        name="analysis",
    )(on_chip(parts), split, mean)
    return update.reshape(background_expectation.shape), analysis.reshape(factor.shape)


def solution(mesh):
    return jax.shard_map(
        per_device,
        mesh=mesh,
        in_specs=(
            P(None, "lat", "lon"),
            P(None, None, "lat", "lon"),
            P("lat", "lon"),
            P(("lat", "lon")),
            P(("lat", "lon")),
            P(("lat", "lon")),
            P(("lat", "lon")),
        ),
        out_specs=(P(None, "lat", "lon"), P(None, None, "lat", "lon")),
        check_vma=False,
    )
```

```python
import functools

import jax
import jax.numpy as jnp
from jax import lax
from jax.experimental import pallas as pl
from jax.experimental.pallas import tpu as pltpu
from jax.sharding import PartitionSpec as P

STEPS = 4
TIME_STEP = 0.9
ROTATION = 0.25

RANK = 32
ROWS = 8
LANES = 128
HALO = 2 * STEPS
TILES = RANK // 8
PLANES = 3 * ROWS
GROUP = LANES // TILES
MAIN, SMALL, SIDE = 0, 12, 13
PER_ROW = 17
PULL = 0.5 * TIME_STEP
WIDTH = 4
HIGHEST = lax.Precision.HIGHEST
NT = (((1,), (1,)), ((), ()))


def lane_iota():
    return lax.broadcasted_iota(jnp.int32, (8, LANES), 1)


def member_rows(field, row, tile):
    return pl.ds(8 * tile * PLANES + field * ROWS + row, 8, stride=PLANES)


def block_at(row, tile):
    return pl.ds((row * PER_ROW + tile) * 8, 8)


def pack_kernel(factor_ref, mean_ref, depth_ref, block_ref, edge_ref):
    lane = lane_iota()
    part = lane // GROUP
    even = ((lane - 8) & 16) == 0
    kept = {}
    for row in range(ROWS):
        small = jnp.concatenate(
            [mean_ref[f * ROWS + row : f * ROWS + row + 1, :] for f in range(3)]
            + [depth_ref[row : row + 1, :]] * 5,
            0,
        )
        block_ref[block_at(row, SMALL), :] = small
        sides = []
        for field in range(3):
            side = None
            for tile in range(TILES):
                value = factor_ref[member_rows(field, row, tile), :]
                block_ref[block_at(row, MAIN + TILES * field + tile), :] = value
                moved = pltpu.roll(value, 16 + GROUP * tile, 1)
                side = moved if side is None else jnp.where(part == tile, moved, side)
            sides.append(side)
        side = pltpu.roll(small, 16, 1)
        side = jnp.where(part == 0, side, pltpu.roll(side, GROUP, 1))
        sides.append(jnp.where(part < 2, side, pltpu.roll(side, 2 * GROUP, 1)))
        for which, side in enumerate(sides):
            block_ref[block_at(row, SIDE + which), :] = side
            if row % 2 == 0:
                kept[which] = side
            else:
                at = pl.ds(((row // 2) * 4 + which) * 8, 8)
                edge_ref[at, :] = jnp.where(even, kept[which], pltpu.roll(side, 16, 1))


def pulls():
    band = lax.axis_index("lat")
    bands = lax.axis_size("lat")
    north = jnp.where(band > 0, PULL, 0.0)
    south = jnp.where(band < bands - 1, PULL, 0.0)
    return north, south


def lon_difference(value):
    return pltpu.roll(value, LANES - 1, 1) - pltpu.roll(value, 1, 1)


def advance(states, row_pulls):
    north_pull, south_pull = row_pulls
    for step in range(STEPS):
        first, last = 1 + 2 * step, 3 * ROWS - 2 - 2 * step
        for state, depth in states:
            h, e, n = (state.at[field] for field in range(3))
            for row in range(first, last + 1):
                divergence = lon_difference(e[row]) + (n[row + 1] - n[row - 1])
                h[row] = h[row] - depth[row] * divergence
        for state, depth in states:
            h, e, n = (state.at[field] for field in range(3))
            for row in range(first + 1, last):
                row_pull = north_pull if row < ROWS else south_pull if row >= 2 * ROWS else PULL
                east, north = e[row], n[row]
                e[row] = east - PULL * lon_difference(h[row]) + ROTATION * north
                n[row] = north - row_pull * (h[row + 1] - h[row - 1]) - ROTATION * east


def observed(count_ref, cells_ref, values_ref, error_ref):
    slots = cells_ref.shape[1]
    live = lax.broadcasted_iota(jnp.int32, (1, slots), 1) < count_ref[0]
    weight = jnp.where(live, 1.0, 0.0) / error_ref[...]
    square = weight * weight
    cells = cells_ref[...]
    row_of = cells // LANES
    lane_of = cells - row_of * LANES
    in_row = lax.broadcasted_iota(jnp.int32, (ROWS, slots), 0) == row_of
    spread = jnp.concatenate(
        [jnp.where(in_row, square, 0.0), jnp.where(in_row, square * values_ref[...], 0.0)], 0
    )
    in_lane = lax.broadcasted_iota(jnp.int32, (LANES, slots), 0) == lane_of
    return lax.dot_general(
        spread, jnp.where(in_lane, 1.0, 0.0), NT, precision=HIGHEST, preferred_element_type=jnp.float32
    )


def inner_kernel(
    count_ref, own_ref, north_ref, south_ref, cells_ref, values_ref, error_ref, out_ref, weight_ref, state, depth
):
    blocks = (north_ref, own_ref, south_ref)
    for block, ref in enumerate(blocks):
        for row in range(ROWS):
            depth[ROWS * block + row] = PULL * jnp.broadcast_to(
                ref[pl.ds((row * PER_ROW + SMALL) * 8 + 3, 1), :], (8, LANES)
            )
    weight_ref[...] = observed(count_ref, cells_ref, values_ref, error_ref)
    row_pulls = pulls()

    def pair(which, carry):
        for half in range(2):
            tile = 2 * which + half
            for block, ref in enumerate(blocks):
                for field in range(3):
                    for row in range(ROWS):
                        at = pl.multiple_of((row * PER_ROW + MAIN + TILES * field + tile) * 8, 8)
                        state[half, field, ROWS * block + row] = ref[pl.ds(at, 8), :]
        advance([(state.at[half], depth) for half in range(2)], row_pulls)
        for half in range(2):
            tile = 2 * which + half
            for field in range(3):
                for row in range(ROWS):
                    at = pl.multiple_of(((field * ROWS + row) * TILES + tile) * 8, 8)
                    out_ref[pl.ds(at, 8), :] = state[half, field, ROWS + row]
        return carry

    lax.fori_loop(0, TILES // 2, pair, 0)


def side_kernel(
    own_ref, north_ref, south_ref, halo_ref, north_halo_ref, south_halo_ref, inner_ref, weight_ref,
    split_ref, mean_out_ref, gram_ref, state, depth, heights, scaled,
):
    lane = lane_iota()
    low_lanes = (lane & 16) == 0
    sub = lax.broadcasted_iota(jnp.int32, (8, LANES), 0)
    blocks = ((north_ref, north_halo_ref), (own_ref, halo_ref), (south_ref, south_halo_ref))
    for block, (ref, halos) in enumerate(blocks):
        for row in range(ROWS):
            at = ROWS * block + row
            for which in range(4):
                side = ref[block_at(row, SIDE + which), :]
                halo = halos[pl.ds(((row // 2) * 4 + which) * 8, 8), :]
                if row % 2:
                    halo = pltpu.roll(halo, LANES - 16, 1)
                right = jnp.where(low_lanes, side, halo)
                left = jnp.where(low_lanes, halo, side)
                if which < 3:
                    state[0, which, at] = right
                    state[1, which, at] = left
                else:
                    small = ref[block_at(row, SMALL), :]
                    for field in range(3):
                        state[2, field, at] = jnp.where(
                            sub == 0,
                            jnp.broadcast_to(small[field : field + 1, :], (8, LANES)),
                            jnp.where(
                                sub == 1,
                                jnp.broadcast_to(right[field : field + 1, :], (8, LANES)),
                                jnp.broadcast_to(left[field : field + 1, :], (8, LANES)),
                            ),
                        )
                    depth[0, at] = PULL * jnp.broadcast_to(right[3:4, :], (8, LANES))
                    depth[1, at] = PULL * jnp.broadcast_to(left[3:4, :], (8, LANES))
                    whole = PULL * jnp.broadcast_to(small[3:4, :], (8, LANES))
                    depth[2, at] = jnp.where(sub == 0, whole, jnp.where(sub == 1, depth[0, at], depth[1, at]))
    advance([(state.at[which], depth.at[which]) for which in range(3)], pulls())

    from_right = (lane & 16) == 0
    edge = (lane < HALO) | (lane >= LANES - HALO)
    for field in range(3):
        for row in range(ROWS):
            plane = field * ROWS + row
            cols = slice(plane * LANES, (plane + 1) * LANES)
            sides = jnp.where(from_right, state[0, field, ROWS + row], state[1, field, ROWS + row])
            full = jnp.concatenate(
                [
                    jnp.where(
                        edge,
                        pltpu.roll(sides, (LANES - 16 - GROUP * tile) % LANES, 1),
                        inner_ref[pl.ds((plane * TILES + tile) * 8, 8), :],
                    )
                    for tile in range(TILES)
                ],
                0,
            )
            high = full.astype(jnp.bfloat16)
            rest = full - high.astype(jnp.float32)
            middle = rest.astype(jnp.bfloat16)
            split_ref[0:RANK, cols] = high
            split_ref[RANK : 2 * RANK, cols] = middle
            split_ref[2 * RANK : 3 * RANK, cols] = (rest - middle.astype(jnp.float32)).astype(jnp.bfloat16)
            mine = state[2, field, ROWS + row]
            both = jnp.where(from_right[0:1], mine[1:2, :], mine[2:3, :])
            mean = jnp.where(edge[0:1], pltpu.roll(both, LANES - 16, 1), mine[0:1, :])
            mean_out_ref[plane : plane + 1, :] = mean
            if field == 0:
                square = weight_ref[row : row + 1, :]
                heights[:, cols] = full
                scaled[0:RANK, cols] = full * square
                pulled = weight_ref[ROWS + row : ROWS + row + 1, :] - square * mean
                scaled[RANK : RANK + 8, cols] = jnp.broadcast_to(pulled, (8, LANES))
    gram = lax.dot_general(
        heights[...], scaled[...], NT, precision=HIGHEST, preferred_element_type=jnp.float32
    )
    gram = jnp.concatenate([gram, jnp.zeros((RANK, LANES - RANK - 8), jnp.float32)], 1)
    acc = None
    for tile in range(TILES):
        part = gram[8 * tile : 8 * tile + 8, :]
        if tile < 2:
            far = gram[8 * tile + 16 : 8 * tile + 24, :]
            part = jnp.where(lane == 31, pltpu.roll(part, LANES - 1, 1), part)
            part = jnp.where(lane == 30, pltpu.roll(far, LANES - 2, 1), part)
        moved = pltpu.roll(part, 32 * tile, 1) if tile else part
        acc = moved if acc is None else jnp.where(lane // 32 == tile, moved, acc)
    gram_ref[...] = acc


def analysis_kernel(parts_ref, split_ref, mean_ref, update_ref, factor_ref):
    lane = lane_iota()
    total = jnp.sum(parts_ref[...], 0)
    tiles, drives = [], [None] * TILES
    for tile in range(TILES):
        part = pltpu.roll(total, LANES - 32 * tile, 1) if tile else total
        if tile < 2:
            drives[tile] = pltpu.roll(part, 2 * RANK - 31, 1)
            drives[tile + 2] = pltpu.roll(part, 2 * RANK - 30, 1)
        tiles.append(part)
    lower = jnp.concatenate(tiles, 0)
    wide = lax.broadcasted_iota(jnp.int32, (RANK, LANES), 1)
    deep = lax.broadcasted_iota(jnp.int32, (RANK, LANES), 0)
    mirrored = jnp.concatenate([lower, jnp.zeros((LANES - RANK, LANES), jnp.float32)], 0).T[0:RANK, :]
    work = jnp.where(wide > deep, mirrored, lower)
    work = jnp.where(wide < RANK, work, 0.0) + jnp.where((wide == deep) | (wide == deep + RANK), 1.0, 0.0)
    work = jnp.where(wide == 2 * RANK, jnp.concatenate(drives, 0), work)
    for first in range(0, RANK, WIDTH):
        columns = [jnp.broadcast_to(work[:, k : k + 1], (RANK, LANES)) for k in range(first, first + WIDTH)]
        rows = [work[k : k + 1, :] for k in range(first, first + WIDTH)]
        for j in range(WIDTH):
            k = first + j
            inverse = 1.0 / columns[j][k : k + 1, :]
            scaled_row = rows[j] * inverse
            for i in range(j + 1, WIDTH):
                ratio = columns[j][first + i : first + i + 1, :] * inverse
                rows[i] = rows[i] - ratio * rows[j]
                columns[i] = columns[i] - columns[j] * ratio
            work = work - jnp.where(deep > k, columns[j], 0.0) * scaled_row
    pivots = jnp.sum(jnp.where(wide == deep, work, 0.0), 1, keepdims=True)
    work = work * lax.rsqrt(pivots)
    shift = jnp.sum(work * work[:, 2 * RANK : 2 * RANK + 1], 0, keepdims=True)
    mixed = jnp.concatenate([work, jnp.broadcast_to(shift, (8, LANES))], 0)[:, RANK : 2 * RANK]
    high = mixed.astype(jnp.bfloat16)
    rest = mixed - high.astype(jnp.float32)
    middle = rest.astype(jnp.bfloat16)
    low = (rest - middle.astype(jnp.float32)).astype(jnp.bfloat16)
    left = jnp.concatenate([high, high, high, middle, middle, low], 1)
    split = split_ref[...]
    fine = jnp.concatenate([split, split[0 : 2 * RANK], split[0:RANK]], 0)
    out = jnp.dot(left, fine, preferred_element_type=jnp.float32)
    for plane in range(PLANES):
        cols = slice(plane * LANES, (plane + 1) * LANES)
        for tile in range(TILES):
            factor_ref[pl.ds(8 * tile * PLANES + plane, 8, stride=PLANES), :] = out[8 * tile : 8 * tile + 8, cols]
        update_ref[plane : plane + 1, :] = mean_ref[plane : plane + 1, :] + out[RANK : RANK + 1, cols]


VMEM = pl.BlockSpec(memory_space=pltpu.VMEM)
SMEM = pl.BlockSpec(memory_space=pltpu.SMEM)


def f32(*shape):
    return jax.ShapeDtypeStruct(shape, jnp.float32)


def chip(*shape):
    return pltpu.VMEM(shape, jnp.float32)


def on_chip(value):
    return pltpu.with_memory_space_constraint(value, pltpu.VMEM)


def shift_by(value, axis, step, periodic):
    count = lax.axis_size(axis)
    pairs = [(i, (i + step) % count) for i in range(count) if periodic or 0 <= i + step < count]
    return lax.ppermute(value, axis, pairs)


def sum_over(value, axis):
    count = lax.axis_size(axis)
    sent = jnp.broadcast_to(value[None], (count, *value.shape))
    return lax.all_to_all(sent, axis, 0, 0)


def per_device(
    background_expectation, factor, average_thickness, obs_cells, obs_count, obs_values, obs_error
):
    assert factor.shape == (RANK, 3, ROWS, LANES)
    block, edges = pl.pallas_call(
        pack_kernel,
        out_shape=(chip(ROWS * PER_ROW * 8, LANES), chip(ROWS * 16, LANES)),
        in_specs=[VMEM] * 3,
        out_specs=(VMEM, VMEM),
        name="pack",
    )(factor.reshape(RANK * PLANES, LANES), background_expectation.reshape(PLANES, LANES), average_thickness)
    block = on_chip(block)
    from_west = shift_by(edges, "lon", 1, True)
    from_east = shift_by(edges, "lon", -1, True)
    north = on_chip(shift_by(block, "lat", 1, False))
    south = on_chip(shift_by(block, "lat", -1, False))
    east_lane = (lax.broadcasted_iota(jnp.int32, (ROWS * 16, LANES), 1) & 8) == 0
    halo = jnp.where(east_lane, from_east, from_west)
    north_halo = on_chip(shift_by(halo, "lat", 1, False))
    south_halo = on_chip(shift_by(halo, "lat", -1, False))
    slots = obs_cells.shape[0]
    inner, weights = pl.pallas_call(
        inner_kernel,
        out_shape=(chip(RANK * PLANES, LANES), chip(2 * ROWS, LANES)),
        in_specs=[SMEM] + [VMEM] * 6,
        out_specs=(VMEM, VMEM),
        scratch_shapes=[
            pltpu.VMEM((2, 3, 3 * ROWS, 8, LANES), jnp.float32),
            pltpu.VMEM((3 * ROWS, 8, LANES), jnp.float32),
        ],
        name="inner",
    )(
        obs_count, block, north, south,
        obs_cells.reshape(1, slots), obs_values.reshape(1, slots), obs_error.reshape(1, slots),
    )
    split, mean, gram = pl.pallas_call(
        side_kernel,
        out_shape=(
            pltpu.VMEM((3 * RANK, PLANES * LANES), jnp.bfloat16),
            chip(PLANES, LANES),
            chip(8, LANES),
        ),
        in_specs=[VMEM] * 8,
        out_specs=(VMEM,) * 3,
        scratch_shapes=[
            pltpu.VMEM((3, 3, 3 * ROWS, 8, LANES), jnp.float32),
            pltpu.VMEM((3, 3 * ROWS, 8, LANES), jnp.float32),
            pltpu.VMEM((RANK, ROWS * LANES), jnp.float32),
            pltpu.VMEM((RANK + 8, ROWS * LANES), jnp.float32),
        ],
        name="side",
    )(block, north, south, on_chip(halo), north_halo, south_halo, on_chip(inner), on_chip(weights))
    gram = jnp.sum(sum_over(gram, "lat"), 0)
    parts = sum_over(gram, "lon")
    update, analysis = pl.pallas_call(
        analysis_kernel,
        out_shape=(f32(PLANES, LANES), f32(RANK * PLANES, LANES)),
        in_specs=[VMEM] * 3,
        out_specs=(VMEM, VMEM),
        name="analysis",
    )(on_chip(parts), on_chip(split), on_chip(mean))
    return update.reshape(background_expectation.shape), analysis.reshape(factor.shape)


def solution(mesh):
    return jax.shard_map(
        per_device,
        mesh=mesh,
        in_specs=(
            P(None, "lat", "lon"),
            P(None, None, "lat", "lon"),
            P("lat", "lon"),
            P(("lat", "lon")),
            P(("lat", "lon")),
            P(("lat", "lon")),
            P(("lat", "lon")),
        ),
        out_specs=(P(None, "lat", "lon"), P(None, None, "lat", "lon")),
        check_vma=False,
    )
```

```python
import jax
import jax.numpy as jnp
from jax import lax
from jax.experimental import pallas as pl
from jax.experimental.pallas import tpu as pltpu
from jax.sharding import PartitionSpec as P


STEPS = 4
TIME_STEP = 0.9
ROTATION = 0.25

RANK = 32
ROWS = 8
LANES = 128
HALO = 2 * STEPS
TILES = RANK // 8
PLANES = 3 * ROWS
GROUP = LANES // TILES
MAIN, SMALL, SIDE = 0, 12, 13
PER_ROW = 17
PULL = 0.5 * TIME_STEP
WIDTH = 4
HIGHEST = lax.Precision.HIGHEST
NT = (((1,), (1,)), ((), ()))


def lane_iota():
    return lax.broadcasted_iota(jnp.int32, (8, LANES), 1)


def member_rows(field, row, tile):
    return pl.ds(8 * tile * PLANES + field * ROWS + row, 8, stride=PLANES)


def block_at(row, tile):
    return pl.ds((row * PER_ROW + tile) * 8, 8)


def pack_kernel(factor_ref, mean_ref, depth_ref, block_ref, edge_ref):
    lane = lane_iota()
    part = lane // GROUP
    even = ((lane - 8) & 16) == 0
    kept = {}
    for row in range(ROWS):
        small = jnp.concatenate(
            [mean_ref[f * ROWS + row : f * ROWS + row + 1, :] for f in range(3)]
            + [depth_ref[row : row + 1, :]] * 5,
            0,
        )
        block_ref[block_at(row, SMALL), :] = small
        sides = []
        for field in range(3):
            side = None
            for tile in range(TILES):
                value = factor_ref[member_rows(field, row, tile), :]
                block_ref[block_at(row, MAIN + TILES * field + tile), :] = value
                moved = pltpu.roll(value, 16 + GROUP * tile, 1)
                side = moved if side is None else jnp.where(part == tile, moved, side)
            sides.append(side)
        side = pltpu.roll(small, 16, 1)
        side = jnp.where(part == 0, side, pltpu.roll(side, GROUP, 1))
        sides.append(jnp.where(part < 2, side, pltpu.roll(side, 2 * GROUP, 1)))
        for which, side in enumerate(sides):
            block_ref[block_at(row, SIDE + which), :] = side
            if row % 2 == 0:
                kept[which] = side
            else:
                at = pl.ds(((row // 2) * 4 + which) * 8, 8)
                edge_ref[at, :] = jnp.where(even, kept[which], pltpu.roll(side, 16, 1))


def pulls():
    band = lax.axis_index("lat")
    bands = lax.axis_size("lat")
    north = jnp.where(band > 0, PULL, 0.0)
    south = jnp.where(band < bands - 1, PULL, 0.0)
    return north, south


def by_side(near, far):
    odd = lax.rem(lax.axis_index("lat"), 2) == 1
    return jnp.where(odd, near, far), jnp.where(odd, far, near)


def lon_difference(value):
    return pltpu.roll(value, LANES - 1, 1) - pltpu.roll(value, 1, 1)


def advance(states, row_pulls):
    north_pull, south_pull = row_pulls
    for step in range(STEPS):
        first, last = 1 + 2 * step, 3 * ROWS - 2 - 2 * step
        for state, depth in states:
            h, e, n = (state.at[field] for field in range(3))
            for row in range(first, last + 1):
                divergence = lon_difference(e[row]) + (n[row + 1] - n[row - 1])
                h[row] = h[row] - depth[row] * divergence
        for state, depth in states:
            h, e, n = (state.at[field] for field in range(3))
            for row in range(first + 1, last):
                row_pull = north_pull if row < ROWS else south_pull if row >= 2 * ROWS else PULL
                east, north = e[row], n[row]
                e[row] = east - PULL * lon_difference(h[row]) + ROTATION * north
                n[row] = north - row_pull * (h[row + 1] - h[row - 1]) - ROTATION * east


def observed(count_ref, cells_ref, values_ref, error_ref):
    slots = cells_ref.shape[1]
    live = lax.broadcasted_iota(jnp.int32, (1, slots), 1) < count_ref[0]
    weight = jnp.where(live, 1.0, 0.0) / error_ref[...]
    square = weight * weight
    cells = cells_ref[...]
    row_of = cells // LANES
    lane_of = cells - row_of * LANES
    in_row = lax.broadcasted_iota(jnp.int32, (ROWS, slots), 0) == row_of
    spread = jnp.concatenate(
        [jnp.where(in_row, square, 0.0), jnp.where(in_row, square * values_ref[...], 0.0)], 0
    )
    in_lane = lax.broadcasted_iota(jnp.int32, (LANES, slots), 0) == lane_of
    return lax.dot_general(
        spread, jnp.where(in_lane, 1.0, 0.0), NT, precision=HIGHEST, preferred_element_type=jnp.float32
    )


def inner_kernel(
    count_ref, own_ref, near_ref, far_ref, cells_ref, values_ref, error_ref, out_ref, weight_ref, state, depth
):
    def around(at):
        north, south = by_side(near_ref[at, :], far_ref[at, :])
        return enumerate((north, own_ref[at, :], south))

    for row in range(ROWS):
        for block, value in around(pl.ds((row * PER_ROW + SMALL) * 8 + 3, 1)):
            depth[ROWS * block + row] = PULL * jnp.broadcast_to(value, (8, LANES))
    weight_ref[...] = observed(count_ref, cells_ref, values_ref, error_ref)
    row_pulls = pulls()

    def pair(which, carry):
        for half in range(2):
            tile = 2 * which + half
            for field in range(3):
                for row in range(ROWS):
                    at = pl.multiple_of((row * PER_ROW + MAIN + TILES * field + tile) * 8, 8)
                    for block, value in around(pl.ds(at, 8)):
                        state[half, field, ROWS * block + row] = value
        advance([(state.at[half], depth) for half in range(2)], row_pulls)
        for half in range(2):
            tile = 2 * which + half
            for field in range(3):
                for row in range(ROWS):
                    at = pl.multiple_of(((field * ROWS + row) * TILES + tile) * 8, 8)
                    out_ref[pl.ds(at, 8), :] = state[half, field, ROWS + row]
        return carry

    lax.fori_loop(0, TILES // 2, pair, 0)


def side_kernel(
    own_ref, near_ref, far_ref, halo_ref, near_halo_ref, far_halo_ref, inner_ref, weight_ref,
    split_ref, mean_out_ref, gram_ref, state, depth, heights, scaled,
):
    lane = lane_iota()
    low_lanes = (lane & 16) == 0
    sub = lax.broadcasted_iota(jnp.int32, (8, LANES), 0)

    def around(own, near, far, at):
        north, south = by_side(near[at, :], far[at, :])
        return north, own[at, :], south

    for row in range(ROWS):
        smalls = around(own_ref, near_ref, far_ref, block_at(row, SMALL))
        for which in range(4):
            sides = around(own_ref, near_ref, far_ref, block_at(row, SIDE + which))
            halos = around(halo_ref, near_halo_ref, far_halo_ref, pl.ds(((row // 2) * 4 + which) * 8, 8))
            for block, (small, side, halo) in enumerate(zip(smalls, sides, halos)):
                at = ROWS * block + row
                if row % 2:
                    halo = pltpu.roll(halo, LANES - 16, 1)
                right = jnp.where(low_lanes, side, halo)
                left = jnp.where(low_lanes, halo, side)
                if which < 3:
                    state[0, which, at] = right
                    state[1, which, at] = left
                    continue
                for field in range(3):
                    state[2, field, at] = jnp.where(
                        sub == 0,
                        jnp.broadcast_to(small[field : field + 1, :], (8, LANES)),
                        jnp.where(
                            sub == 1,
                            jnp.broadcast_to(right[field : field + 1, :], (8, LANES)),
                            jnp.broadcast_to(left[field : field + 1, :], (8, LANES)),
                        ),
                    )
                of_right = PULL * jnp.broadcast_to(right[3:4, :], (8, LANES))
                of_left = PULL * jnp.broadcast_to(left[3:4, :], (8, LANES))
                whole = PULL * jnp.broadcast_to(small[3:4, :], (8, LANES))
                depth[0, at] = of_right
                depth[1, at] = of_left
                depth[2, at] = jnp.where(sub == 0, whole, jnp.where(sub == 1, of_right, of_left))
    advance([(state.at[which], depth.at[which]) for which in range(3)], pulls())

    from_right = (lane & 16) == 0
    edge = (lane < HALO) | (lane >= LANES - HALO)
    for field in range(3):
        for row in range(ROWS):
            plane = field * ROWS + row
            cols = slice(plane * LANES, (plane + 1) * LANES)
            sides = jnp.where(from_right, state[0, field, ROWS + row], state[1, field, ROWS + row])
            full = jnp.concatenate(
                [
                    jnp.where(
                        edge,
                        pltpu.roll(sides, (LANES - 16 - GROUP * tile) % LANES, 1),
                        inner_ref[pl.ds((plane * TILES + tile) * 8, 8), :],
                    )
                    for tile in range(TILES)
                ],
                0,
            )
            high = full.astype(jnp.bfloat16)
            rest = full - high.astype(jnp.float32)
            middle = rest.astype(jnp.bfloat16)
            split_ref[0:RANK, cols] = high
            split_ref[RANK : 2 * RANK, cols] = middle
            split_ref[2 * RANK : 3 * RANK, cols] = (rest - middle.astype(jnp.float32)).astype(jnp.bfloat16)
            mine = state[2, field, ROWS + row]
            both = jnp.where(from_right[0:1], mine[1:2, :], mine[2:3, :])
            mean = jnp.where(edge[0:1], pltpu.roll(both, LANES - 16, 1), mine[0:1, :])
            mean_out_ref[plane : plane + 1, :] = mean
            if field == 0:
                square = weight_ref[row : row + 1, :]
                heights[:, cols] = full
                scaled[0:RANK, cols] = full * square
                pulled = weight_ref[ROWS + row : ROWS + row + 1, :] - square * mean
                scaled[RANK : RANK + 8, cols] = jnp.broadcast_to(pulled, (8, LANES))
    gram = lax.dot_general(
        heights[...], scaled[...], NT, precision=HIGHEST, preferred_element_type=jnp.float32
    )
    gram = jnp.concatenate([gram, jnp.zeros((RANK, LANES - RANK - 8), jnp.float32)], 1)
    acc = None
    for tile in range(TILES):
        part = gram[8 * tile : 8 * tile + 8, :]
        if tile < 2:
            far = gram[8 * tile + 16 : 8 * tile + 24, :]
            part = jnp.where(lane == 31, pltpu.roll(part, LANES - 1, 1), part)
            part = jnp.where(lane == 30, pltpu.roll(far, LANES - 2, 1), part)
        moved = pltpu.roll(part, 32 * tile, 1) if tile else part
        acc = moved if acc is None else jnp.where(lane // 32 == tile, moved, acc)
    gram_ref[...] = acc


def analysis_kernel(parts_ref, split_ref, mean_ref, update_ref, factor_ref):
    lane = lane_iota()
    total = jnp.sum(parts_ref[...], 0)
    tiles, drives = [], [None] * TILES
    for tile in range(TILES):
        part = pltpu.roll(total, LANES - 32 * tile, 1) if tile else total
        if tile < 2:
            drives[tile] = pltpu.roll(part, 2 * RANK - 31, 1)
            drives[tile + 2] = pltpu.roll(part, 2 * RANK - 30, 1)
        tiles.append(part)
    lower = jnp.concatenate(tiles, 0)
    wide = lax.broadcasted_iota(jnp.int32, (RANK, LANES), 1)
    deep = lax.broadcasted_iota(jnp.int32, (RANK, LANES), 0)
    mirrored = jnp.concatenate([lower, jnp.zeros((LANES - RANK, LANES), jnp.float32)], 0).T[0:RANK, :]
    work = jnp.where(wide > deep, mirrored, lower)
    work = jnp.where(wide < RANK, work, 0.0) + jnp.where((wide == deep) | (wide == deep + RANK), 1.0, 0.0)
    work = jnp.where(wide == 2 * RANK, jnp.concatenate(drives, 0), work)
    for first in range(0, RANK, WIDTH):
        columns = [jnp.broadcast_to(work[:, k : k + 1], (RANK, LANES)) for k in range(first, first + WIDTH)]
        rows = [work[k : k + 1, :] for k in range(first, first + WIDTH)]
        for j in range(WIDTH):
            k = first + j
            inverse = 1.0 / columns[j][k : k + 1, :]
            scaled_row = rows[j] * inverse
            for i in range(j + 1, WIDTH):
                ratio = columns[j][first + i : first + i + 1, :] * inverse
                rows[i] = rows[i] - ratio * rows[j]
                columns[i] = columns[i] - columns[j] * ratio
            work = work - jnp.where(deep > k, columns[j], 0.0) * scaled_row
    pivots = jnp.sum(jnp.where(wide == deep, work, 0.0), 1, keepdims=True)
    work = work * lax.rsqrt(pivots)
    shift = jnp.sum(work * work[:, 2 * RANK : 2 * RANK + 1], 0, keepdims=True)
    mixed = jnp.concatenate([work, jnp.broadcast_to(shift, (8, LANES))], 0)[:, RANK : 2 * RANK]
    high = mixed.astype(jnp.bfloat16)
    rest = mixed - high.astype(jnp.float32)
    middle = rest.astype(jnp.bfloat16)
    low = (rest - middle.astype(jnp.float32)).astype(jnp.bfloat16)
    left = jnp.concatenate([high, high, high, middle, middle, low], 1)
    split = split_ref[...]
    fine = jnp.concatenate([split, split[0 : 2 * RANK], split[0:RANK]], 0)
    out = jnp.dot(left, fine, preferred_element_type=jnp.float32)
    for plane in range(PLANES):
        cols = slice(plane * LANES, (plane + 1) * LANES)
        for tile in range(TILES):
            factor_ref[pl.ds(8 * tile * PLANES + plane, 8, stride=PLANES), :] = out[8 * tile : 8 * tile + 8, cols]
        update_ref[plane : plane + 1, :] = mean_ref[plane : plane + 1, :] + out[RANK : RANK + 1, cols]


VMEM = pl.BlockSpec(memory_space=pltpu.VMEM)
SMEM = pl.BlockSpec(memory_space=pltpu.SMEM)


def f32(*shape):
    return jax.ShapeDtypeStruct(shape, jnp.float32)


def chip(*shape):
    return pltpu.VMEM(shape, jnp.float32)


def on_chip(value):
    return pltpu.with_memory_space_constraint(value, pltpu.VMEM)


def swapped(value, axis, offset, periodic):
    count = lax.axis_size(axis)
    pairs = [(i, i + 1) for i in range(offset, count - 1, 2)]
    if offset and periodic:
        pairs.append((count - 1, 0))
    return lax.ppermute(value, axis, pairs + [(j, i) for i, j in pairs])


def sum_over(value, axis):
    count = lax.axis_size(axis)
    sent = jnp.broadcast_to(value[None], (count, *value.shape))
    return lax.all_to_all(sent, axis, 0, 0)


def per_device(
    background_expectation, factor, average_thickness, obs_cells, obs_count, obs_values, obs_error
):
    assert factor.shape == (RANK, 3, ROWS, LANES)
    block, edges = pl.pallas_call(
        pack_kernel,
        out_shape=(chip(ROWS * PER_ROW * 8, LANES), chip(ROWS * 16, LANES)),
        in_specs=[VMEM] * 3,
        out_specs=(VMEM, VMEM),
        name="pack",
    )(factor.reshape(RANK * PLANES, LANES), background_expectation.reshape(PLANES, LANES), average_thickness)
    block = on_chip(block)
    even_edges = swapped(edges, "lon", 0, True)
    odd_edges = swapped(edges, "lon", 1, True)
    far = on_chip(swapped(block, "lat", 1, False))
    near = on_chip(swapped(block, "lat", 0, False))
    eastern = (lax.broadcasted_iota(jnp.int32, (ROWS * 16, LANES), 1) & 8) // 8 != 1
    from_even = eastern == (lax.rem(lax.axis_index("lon"), 2) == 0)
    halo = jnp.where(from_even, even_edges, odd_edges)
    far_halo = on_chip(swapped(halo, "lat", 1, False))
    near_halo = on_chip(swapped(halo, "lat", 0, False))
    slots = obs_cells.shape[0]
    inner, weights = pl.pallas_call(
        inner_kernel,
        out_shape=(chip(RANK * PLANES, LANES), chip(2 * ROWS, LANES)),
        in_specs=[SMEM] + [VMEM] * 6,
        out_specs=(VMEM, VMEM),
        scratch_shapes=[
            pltpu.VMEM((2, 3, 3 * ROWS, 8, LANES), jnp.float32),
            pltpu.VMEM((3 * ROWS, 8, LANES), jnp.float32),
        ],
        name="inner",
    )(
        obs_count, block, near, far,
        obs_cells.reshape(1, slots), obs_values.reshape(1, slots), obs_error.reshape(1, slots),
    )
    split, mean, gram = pl.pallas_call(
        side_kernel,
        out_shape=(
            pltpu.VMEM((3 * RANK, PLANES * LANES), jnp.bfloat16),
            chip(PLANES, LANES),
            chip(8, LANES),
        ),
        in_specs=[VMEM] * 8,
        out_specs=(VMEM,) * 3,
        scratch_shapes=[
            pltpu.VMEM((3, 3, 3 * ROWS, 8, LANES), jnp.float32),
            pltpu.VMEM((3, 3 * ROWS, 8, LANES), jnp.float32),
            pltpu.VMEM((RANK, ROWS * LANES), jnp.float32),
            pltpu.VMEM((RANK + 8, ROWS * LANES), jnp.float32),
        ],
        name="side",
    )(block, near, far, on_chip(halo), near_halo, far_halo, on_chip(inner), on_chip(weights))
    gram = jnp.sum(sum_over(gram, "lat"), 0)
    parts = sum_over(gram, "lon")
    update, analysis = pl.pallas_call(
        analysis_kernel,
        out_shape=(f32(PLANES, LANES), f32(RANK * PLANES, LANES)),
        in_specs=[VMEM] * 3,
        out_specs=(VMEM, VMEM),
        name="analysis",
    )(on_chip(parts), on_chip(split), on_chip(mean))
    return update.reshape(background_expectation.shape), analysis.reshape(factor.shape)


def solution(mesh):
    return jax.shard_map(
        per_device,
        mesh=mesh,
        in_specs=(
            P(None, "lat", "lon"),
            P(None, None, "lat", "lon"),
            P("lat", "lon"),
            P(("lat", "lon")),
            P(("lat", "lon")),
            P(("lat", "lon")),
            P(("lat", "lon")),
        ),
        out_specs=(P(None, "lat", "lon"), P(None, None, "lat", "lon")),
        check_vma=False,
    )
```

```python
import jax
import jax.numpy as jnp
from jax import lax
from jax.experimental import pallas as pl
from jax.experimental.pallas import tpu as pltpu
from jax.sharding import PartitionSpec as P


STEPS = 4
TIME_STEP = 0.9
ROTATION = 0.25

RANK = 32
ROWS = 8
LANES = 128
HALO = 2 * STEPS
TILES = RANK // 8
PLANES = 3 * ROWS
GROUP = LANES // TILES
MAIN, SMALL, SIDE = 0, 12, 13
PER_ROW = 17
MOVES = (0, 16, 8, 24)
PULL = 0.5 * TIME_STEP
WIDTH = 8
HIGHEST = lax.Precision.HIGHEST
NT = (((1,), (1,)), ((), ()))


def lane_iota():
    return lax.broadcasted_iota(jnp.int32, (8, LANES), 1)


def member_rows(field, row, tile):
    return pl.ds(8 * tile * PLANES + field * ROWS + row, 8, stride=PLANES)


def block_at(row, tile):
    return pl.ds((row * PER_ROW + tile) * 8, 8)


def pack_kernel(factor_ref, mean_ref, depth_ref, block_ref, even_edge_ref, odd_edge_ref):
    lane = lane_iota()
    part = lane // GROUP
    octet = (lane // 8) & 3
    even = lax.rem(lax.axis_index("lon"), 2) == 0
    eastward, westward = {}, {}
    for row in range(ROWS):
        small = jnp.concatenate(
            [mean_ref[f * ROWS + row : f * ROWS + row + 1, :] for f in range(3)]
            + [depth_ref[row : row + 1, :]] * 5,
            0,
        )
        block_ref[block_at(row, SMALL), :] = small
        sides = []
        for field in range(3):
            side = None
            for tile in range(TILES):
                value = factor_ref[member_rows(field, row, tile), :]
                block_ref[block_at(row, MAIN + TILES * field + tile), :] = value
                moved = pltpu.roll(value, 16 + GROUP * tile, 1)
                side = moved if side is None else jnp.where(part == tile, moved, side)
            sides.append(side)
        side = pltpu.roll(small, 16, 1)
        side = jnp.where(part == 0, side, pltpu.roll(side, GROUP, 1))
        sides.append(jnp.where(part < 2, side, pltpu.roll(side, 2 * GROUP, 1)))
        for which, side in enumerate(sides):
            block_ref[block_at(row, SIDE + which), :] = side
            move = MOVES[row % 4]
            moved = pltpu.roll(side, move, 1) if move else side
            if row % 4 == 0:
                eastward[which] = westward[which] = moved
                continue
            eastward[which] = jnp.where(octet == (1 + move // 8) % 4, moved, eastward[which])
            westward[which] = jnp.where(octet == (2 + move // 8) % 4, moved, westward[which])
            if row % 4 == 3:
                at = pl.ds(((row // 4) * 4 + which) * 8, 8)
                even_edge_ref[at, :] = jnp.where(even, eastward[which], westward[which])
                odd_edge_ref[at, :] = jnp.where(even, westward[which], eastward[which])


def pulls():
    band = lax.axis_index("lat")
    bands = lax.axis_size("lat")
    north = jnp.where(band > 0, PULL, 0.0)
    south = jnp.where(band < bands - 1, PULL, 0.0)
    return north, south


def by_side(near, far):
    odd = lax.rem(lax.axis_index("lat"), 2) == 1
    return jnp.where(odd, near, far), jnp.where(odd, far, near)


def lon_difference(value):
    return pltpu.roll(value, LANES - 1, 1) - pltpu.roll(value, 1, 1)


def advance(states, row_pulls):
    north_pull, south_pull = row_pulls
    for step in range(STEPS):
        first, last = 1 + 2 * step, 3 * ROWS - 2 - 2 * step
        for state, depth in states:
            h, e, n = (state.at[field] for field in range(3))
            for row in range(first, last + 1):
                divergence = lon_difference(e[row]) + (n[row + 1] - n[row - 1])
                h[row] = h[row] - depth[row] * divergence
        for state, depth in states:
            h, e, n = (state.at[field] for field in range(3))
            for row in range(first + 1, last):
                row_pull = north_pull if row < ROWS else south_pull if row >= 2 * ROWS else PULL
                east, north = e[row], n[row]
                e[row] = east - PULL * lon_difference(h[row]) + ROTATION * north
                n[row] = north - row_pull * (h[row + 1] - h[row - 1]) - ROTATION * east


def weight_kernel(count_ref, cells_ref, values_ref, error_ref, out_ref):
    slots = cells_ref.shape[1]
    live = lax.broadcasted_iota(jnp.int32, (1, slots), 1) < count_ref[...]
    weight = jnp.where(live, 1.0, 0.0) / error_ref[...]
    square = weight * weight
    cells = cells_ref[...]
    row_of = cells // LANES
    lane_of = cells - row_of * LANES
    in_row = lax.broadcasted_iota(jnp.int32, (ROWS, slots), 0) == row_of
    spread = jnp.concatenate(
        [jnp.where(in_row, square, 0.0), jnp.where(in_row, square * values_ref[...], 0.0)], 0
    )
    in_lane = lax.broadcasted_iota(jnp.int32, (LANES, slots), 0) == lane_of
    out_ref[...] = lax.dot_general(
        spread, jnp.where(in_lane, 1.0, 0.0), NT, precision=HIGHEST, preferred_element_type=jnp.float32
    )


def inner_kernel(own_ref, near_ref, far_ref, out_ref, state, depth):
    def around(at):
        north, south = by_side(near_ref[at, :], far_ref[at, :])
        return enumerate((north, own_ref[at, :], south))

    for row in range(ROWS):
        for block, value in around(pl.ds((row * PER_ROW + SMALL) * 8 + 3, 1)):
            depth[ROWS * block + row] = PULL * jnp.broadcast_to(value, (8, LANES))
    row_pulls = pulls()

    def pair(which, carry):
        for half in range(2):
            tile = 2 * which + half
            for field in range(3):
                for row in range(ROWS):
                    at = pl.multiple_of((row * PER_ROW + MAIN + TILES * field + tile) * 8, 8)
                    for block, value in around(pl.ds(at, 8)):
                        state[half, field, ROWS * block + row] = value
        advance([(state.at[half], depth) for half in range(2)], row_pulls)
        for half in range(2):
            tile = 2 * which + half
            for field in range(3):
                for row in range(ROWS):
                    at = pl.multiple_of(((field * ROWS + row) * TILES + tile) * 8, 8)
                    out_ref[pl.ds(at, 8), :] = state[half, field, ROWS + row]
        return carry

    lax.fori_loop(0, TILES // 2, pair, 0)


def side_kernel(
    own_ref, near_ref, far_ref, halo_ref, near_halo_ref, far_halo_ref, inner_ref, weight_ref,
    split_ref, mean_out_ref, gram_ref, state, depth, heights, scaled,
):
    lane = lane_iota()
    low_lanes = (lane & 16) == 0
    sub = lax.broadcasted_iota(jnp.int32, (8, LANES), 0)

    def around(own, near, far, at):
        north, south = by_side(near[at, :], far[at, :])
        return north, own[at, :], south

    for row in range(ROWS):
        smalls = around(own_ref, near_ref, far_ref, block_at(row, SMALL))
        for which in range(4):
            sides = around(own_ref, near_ref, far_ref, block_at(row, SIDE + which))
            halos = around(halo_ref, near_halo_ref, far_halo_ref, pl.ds(((row // 2) * 4 + which) * 8, 8))
            for block, (small, side, halo) in enumerate(zip(smalls, sides, halos)):
                at = ROWS * block + row
                if MOVES[row % 4]:
                    halo = pltpu.roll(halo, LANES - MOVES[row % 4], 1)
                right = jnp.where(low_lanes, side, halo)
                left = jnp.where(low_lanes, halo, side)
                if which < 3:
                    state[0, which, at] = right
                    state[1, which, at] = left
                    continue
                for field in range(3):
                    state[2, field, at] = jnp.where(
                        sub == 0,
                        jnp.broadcast_to(small[field : field + 1, :], (8, LANES)),
                        jnp.where(
                            sub == 1,
                            jnp.broadcast_to(right[field : field + 1, :], (8, LANES)),
                            jnp.broadcast_to(left[field : field + 1, :], (8, LANES)),
                        ),
                    )
                of_right = PULL * jnp.broadcast_to(right[3:4, :], (8, LANES))
                of_left = PULL * jnp.broadcast_to(left[3:4, :], (8, LANES))
                whole = PULL * jnp.broadcast_to(small[3:4, :], (8, LANES))
                depth[0, at] = of_right
                depth[1, at] = of_left
                depth[2, at] = jnp.where(sub == 0, whole, jnp.where(sub == 1, of_right, of_left))
    advance([(state.at[which], depth.at[which]) for which in range(3)], pulls())

    from_right = (lane & 16) == 0
    edge = (lane < HALO) | (lane >= LANES - HALO)
    for field in range(3):
        for row in range(ROWS):
            plane = field * ROWS + row
            cols = slice(plane * LANES, (plane + 1) * LANES)
            sides = jnp.where(from_right, state[0, field, ROWS + row], state[1, field, ROWS + row])
            full = jnp.concatenate(
                [
                    jnp.where(
                        edge,
                        pltpu.roll(sides, (LANES - 16 - GROUP * tile) % LANES, 1),
                        inner_ref[pl.ds((plane * TILES + tile) * 8, 8), :],
                    )
                    for tile in range(TILES)
                ],
                0,
            )
            high = full.astype(jnp.bfloat16)
            rest = full - high.astype(jnp.float32)
            middle = rest.astype(jnp.bfloat16)
            split_ref[0:RANK, cols] = high
            split_ref[RANK : 2 * RANK, cols] = middle
            split_ref[2 * RANK : 3 * RANK, cols] = (rest - middle.astype(jnp.float32)).astype(jnp.bfloat16)
            mine = state[2, field, ROWS + row]
            both = jnp.where(from_right[0:1], mine[1:2, :], mine[2:3, :])
            mean = jnp.where(edge[0:1], pltpu.roll(both, LANES - 16, 1), mine[0:1, :])
            mean_out_ref[plane : plane + 1, :] = mean
            if field == 0:
                square = weight_ref[row : row + 1, :]
                heights[:, cols] = full
                scaled[0:RANK, cols] = full * square
                pulled = weight_ref[ROWS + row : ROWS + row + 1, :] - square * mean
                scaled[RANK : RANK + 8, cols] = jnp.broadcast_to(pulled, (8, LANES))
    gram = lax.dot_general(
        heights[...], scaled[...], NT, precision=HIGHEST, preferred_element_type=jnp.float32
    )
    gram = jnp.concatenate([gram, jnp.zeros((RANK, LANES - RANK - 8), jnp.float32)], 1)
    acc = None
    for tile in range(TILES):
        part = gram[8 * tile : 8 * tile + 8, :]
        if tile < 2:
            far = gram[8 * tile + 16 : 8 * tile + 24, :]
            part = jnp.where(lane == 31, pltpu.roll(part, LANES - 1, 1), part)
            part = jnp.where(lane == 30, pltpu.roll(far, LANES - 2, 1), part)
        moved = pltpu.roll(part, 32 * tile, 1) if tile else part
        acc = moved if acc is None else jnp.where(lane // 32 == tile, moved, acc)
    gram_ref[...] = acc


def analysis_kernel(parts_ref, split_ref, mean_ref, update_ref, factor_ref):
    lane = lane_iota()
    total = jnp.sum(parts_ref[...], 0)
    tiles, drives = [], [None] * TILES
    for tile in range(TILES):
        part = pltpu.roll(total, LANES - 32 * tile, 1) if tile else total
        if tile < 2:
            drives[tile] = pltpu.roll(part, 2 * RANK - 31, 1)
            drives[tile + 2] = pltpu.roll(part, 2 * RANK - 30, 1)
        tiles.append(part)
    lower = jnp.concatenate(tiles, 0)
    wide = lax.broadcasted_iota(jnp.int32, (RANK, LANES), 1)
    deep = lax.broadcasted_iota(jnp.int32, (RANK, LANES), 0)
    mirrored = jnp.concatenate([lower, jnp.zeros((LANES - RANK, LANES), jnp.float32)], 0).T[0:RANK, :]
    work = jnp.where(wide > deep, mirrored, lower)
    work = jnp.where(wide < RANK, work, 0.0) + jnp.where((wide == deep) | (wide == deep + RANK), 1.0, 0.0)
    work = jnp.where(wide == 2 * RANK, jnp.concatenate(drives, 0), work)
    for first in range(0, RANK, WIDTH):
        columns = [jnp.broadcast_to(work[:, k : k + 1], (RANK, LANES)) for k in range(first, first + WIDTH)]
        rows = [work[k : k + 1, :] for k in range(first, first + WIDTH)]
        for j in range(WIDTH):
            k = first + j
            inverse = 1.0 / columns[j][k : k + 1, :]
            scaled_row = rows[j] * inverse
            for i in range(j + 1, WIDTH):
                ratio = columns[j][first + i : first + i + 1, :] * inverse
                rows[i] = rows[i] - ratio * rows[j]
                columns[i] = columns[i] - columns[j] * ratio
            work = work - jnp.where(deep > k, columns[j], 0.0) * scaled_row
    pivots = jnp.sum(jnp.where(wide == deep, work, 0.0), 1, keepdims=True)
    work = work * lax.rsqrt(pivots)
    shift = jnp.sum(work * work[:, 2 * RANK : 2 * RANK + 1], 0, keepdims=True)
    mixed = jnp.concatenate([work, jnp.broadcast_to(shift, (8, LANES))], 0)[:, RANK : 2 * RANK]
    high = mixed.astype(jnp.bfloat16)
    rest = mixed - high.astype(jnp.float32)
    middle = rest.astype(jnp.bfloat16)
    low = (rest - middle.astype(jnp.float32)).astype(jnp.bfloat16)
    left = jnp.concatenate([high, high, high, middle, middle, low], 1)
    split = split_ref[...]
    fine = jnp.concatenate([split, split[0 : 2 * RANK], split[0:RANK]], 0)
    out = jnp.dot(left, fine, preferred_element_type=jnp.float32)
    for plane in range(PLANES):
        cols = slice(plane * LANES, (plane + 1) * LANES)
        for tile in range(TILES):
            factor_ref[pl.ds(8 * tile * PLANES + plane, 8, stride=PLANES), :] = out[8 * tile : 8 * tile + 8, cols]
        update_ref[plane : plane + 1, :] = mean_ref[plane : plane + 1, :] + out[RANK : RANK + 1, cols]


VMEM = pl.BlockSpec(memory_space=pltpu.VMEM)
SMALL_VMEM = pltpu.CompilerParams(vmem_limit_bytes=8 << 20)


def f32(*shape):
    return jax.ShapeDtypeStruct(shape, jnp.float32)


def chip(*shape):
    return pltpu.VMEM(shape, jnp.float32)


def on_chip(value):
    return pltpu.with_memory_space_constraint(value, pltpu.VMEM)


def swapped(value, axis, offset, periodic):
    count = lax.axis_size(axis)
    pairs = [(i, i + 1) for i in range(offset, count - 1, 2)]
    if offset and periodic:
        pairs.append((count - 1, 0))
    return lax.ppermute(value, axis, pairs + [(j, i) for i, j in pairs])


def sum_over(value, axis):
    count = lax.axis_size(axis)
    sent = jnp.broadcast_to(value[None], (count, *value.shape))
    return lax.all_to_all(sent, axis, 0, 0)


def per_device(
    background_expectation, factor, average_thickness, obs_cells, obs_count, obs_values, obs_error
):
    assert factor.shape == (RANK, 3, ROWS, LANES)
    block, even_edges, odd_edges = pl.pallas_call(
        pack_kernel,
        out_shape=(chip(ROWS * PER_ROW * 8, LANES),) + (chip(ROWS * 8, LANES),) * 2,
        in_specs=[VMEM] * 3,
        out_specs=(VMEM,) * 3,
        name="pack", compiler_params=SMALL_VMEM,
    )(factor.reshape(RANK * PLANES, LANES), background_expectation.reshape(PLANES, LANES), average_thickness)
    block = on_chip(block)
    even_edges = swapped(even_edges, "lon", 0, True)
    odd_edges = swapped(odd_edges, "lon", 1, True)
    far = on_chip(swapped(block, "lat", 1, False))
    near = on_chip(swapped(block, "lat", 0, False))
    slots = obs_cells.shape[0]
    weights = pl.pallas_call(
        weight_kernel, out_shape=chip(2 * ROWS, LANES), in_specs=[VMEM] * 4, out_specs=VMEM, name="weigh", compiler_params=SMALL_VMEM
    )(
        obs_count.reshape(1, 1), obs_cells.reshape(1, slots),
        obs_values.reshape(1, slots), obs_error.reshape(1, slots),
    )
    shape = (ROWS // 4, 4 * 8, LANES)
    eastern = (lax.broadcasted_iota(jnp.int32, shape, 2) & 8) // 8 != 1
    from_even = eastern == (lax.rem(lax.axis_index("lon"), 2) == 0)
    even_edges, odd_edges = even_edges.reshape(shape), odd_edges.reshape(shape)
    halo = jnp.stack(
        [jnp.where(from_even, even_edges, odd_edges), jnp.where(from_even, odd_edges, even_edges)], 1
    ).reshape(ROWS * 16, LANES)
    far_halo = on_chip(swapped(halo, "lat", 1, False))
    near_halo = on_chip(swapped(halo, "lat", 0, False))
    inner = pl.pallas_call(
        inner_kernel,
        out_shape=chip(RANK * PLANES, LANES),
        in_specs=[VMEM] * 3,
        out_specs=VMEM,
        scratch_shapes=[
            pltpu.VMEM((2, 3, 3 * ROWS, 8, LANES), jnp.float32),
            pltpu.VMEM((3 * ROWS, 8, LANES), jnp.float32),
        ],
        name="inner", compiler_params=SMALL_VMEM,
    )(block, near, far)
    split, mean, gram = pl.pallas_call(
        side_kernel,
        out_shape=(
            pltpu.VMEM((3 * RANK, PLANES * LANES), jnp.bfloat16),
            chip(PLANES, LANES),
            chip(8, LANES),
        ),
        in_specs=[VMEM] * 8,
        out_specs=(VMEM,) * 3,
        scratch_shapes=[
            pltpu.VMEM((3, 3, 3 * ROWS, 8, LANES), jnp.float32),
            pltpu.VMEM((3, 3 * ROWS, 8, LANES), jnp.float32),
            pltpu.VMEM((RANK, ROWS * LANES), jnp.float32),
            pltpu.VMEM((RANK + 8, ROWS * LANES), jnp.float32),
        ],
        name="side", compiler_params=SMALL_VMEM,
    )(block, near, far, on_chip(halo), near_halo, far_halo, on_chip(inner), on_chip(weights))
    gram = jnp.sum(sum_over(gram, "lat"), 0)
    parts = sum_over(gram, "lon")
    update, analysis = pl.pallas_call(
        analysis_kernel,
        out_shape=(f32(PLANES, LANES), f32(RANK * PLANES, LANES)),
        in_specs=[VMEM] * 3,
        out_specs=(VMEM, VMEM),
        name="analysis", compiler_params=SMALL_VMEM,
    )(on_chip(parts), on_chip(split), on_chip(mean))
    return update.reshape(background_expectation.shape), analysis.reshape(factor.shape)


def solution(mesh):
    return jax.shard_map(
        per_device,
        mesh=mesh,
        in_specs=(
            P(None, "lat", "lon"),
            P(None, None, "lat", "lon"),
            P("lat", "lon"),
            P(("lat", "lon")),
            P(("lat", "lon")),
            P(("lat", "lon")),
            P(("lat", "lon")),
        ),
        out_specs=(P(None, "lat", "lon"), P(None, None, "lat", "lon")),
        check_vma=False,
    )
```

```python
import jax
import jax.numpy as jnp
from jax import lax
from jax.experimental import pallas as pl
from jax.experimental.pallas import tpu as pltpu
from jax.sharding import PartitionSpec as P


STEPS = 4
TIME_STEP = 0.9
ROTATION = 0.25

RANK = 32
ROWS = 8
LANES = 128
HALO = 2 * STEPS
TILES = RANK // 8
PLANES = 3 * ROWS
GROUP = LANES // TILES
MAIN, SMALL, SIDE = 0, 12, 13
PER_ROW = 17
MOVES = (0, 16, 8, 24)
PULL = 0.5 * TIME_STEP
WIDTH = 8
HIGHEST = lax.Precision.HIGHEST
NT = (((1,), (1,)), ((), ()))


def lane_iota():
    return lax.broadcasted_iota(jnp.int32, (8, LANES), 1)


def member_rows(field, row, tile):
    return pl.ds(8 * tile * PLANES + field * ROWS + row, 8, stride=PLANES)


def block_at(row, tile):
    return pl.ds((row * PER_ROW + tile) * 8, 8)


def observed(count_ref, cells_ref, values_ref, error_ref):
    slots = cells_ref.shape[1]
    live = lax.broadcasted_iota(jnp.int32, (1, slots), 1) < count_ref[...]
    weight = jnp.where(live, 1.0, 0.0) / error_ref[...]
    square = weight * weight
    cells = cells_ref[...]
    row_of = cells // LANES
    lane_of = cells - row_of * LANES
    in_row = lax.broadcasted_iota(jnp.int32, (ROWS, slots), 0) == row_of
    spread = jnp.concatenate(
        [jnp.where(in_row, square, 0.0), jnp.where(in_row, square * values_ref[...], 0.0)], 0
    )
    in_lane = lax.broadcasted_iota(jnp.int32, (LANES, slots), 0) == lane_of
    return lax.dot_general(
        spread, jnp.where(in_lane, 1.0, 0.0), NT, precision=HIGHEST, preferred_element_type=jnp.float32
    )


def pack_kernel(
    factor_ref, mean_ref, depth_ref, count_ref, cells_ref, values_ref, error_ref,
    block_ref, even_edge_ref, odd_edge_ref, weight_ref,
):
    lane = lane_iota()
    part = lane // GROUP
    octet = (lane // 8) & 3
    weight_ref[...] = observed(count_ref, cells_ref, values_ref, error_ref)
    even = lax.rem(lax.axis_index("lon"), 2) == 0
    eastward, westward = {}, {}
    for row in range(ROWS):
        small = jnp.concatenate(
            [mean_ref[f * ROWS + row : f * ROWS + row + 1, :] for f in range(3)]
            + [depth_ref[row : row + 1, :]] * 5,
            0,
        )
        block_ref[block_at(row, SMALL), :] = small
        sides = []
        for field in range(3):
            side = None
            for tile in range(TILES):
                value = factor_ref[member_rows(field, row, tile), :]
                block_ref[block_at(row, MAIN + TILES * field + tile), :] = value
                moved = pltpu.roll(value, 16 + GROUP * tile, 1)
                side = moved if side is None else jnp.where(part == tile, moved, side)
            sides.append(side)
        side = pltpu.roll(small, 16, 1)
        side = jnp.where(part == 0, side, pltpu.roll(side, GROUP, 1))
        sides.append(jnp.where(part < 2, side, pltpu.roll(side, 2 * GROUP, 1)))
        for which, side in enumerate(sides):
            block_ref[block_at(row, SIDE + which), :] = side
            move = MOVES[row % 4]
            moved = pltpu.roll(side, move, 1) if move else side
            if row % 4 == 0:
                eastward[which] = westward[which] = moved
                continue
            eastward[which] = jnp.where(octet == (1 + move // 8) % 4, moved, eastward[which])
            westward[which] = jnp.where(octet == (2 + move // 8) % 4, moved, westward[which])
            if row % 4 == 3:
                at = pl.ds(((row // 4) * 4 + which) * 8, 8)
                even_edge_ref[at, :] = jnp.where(even, eastward[which], westward[which])
                odd_edge_ref[at, :] = jnp.where(even, westward[which], eastward[which])


def pulls():
    band = lax.axis_index("lat")
    bands = lax.axis_size("lat")
    north = jnp.where(band > 0, PULL, 0.0)
    south = jnp.where(band < bands - 1, PULL, 0.0)
    return north, south


def by_side(near, far):
    odd = lax.rem(lax.axis_index("lat"), 2) == 1
    return jnp.where(odd, near, far), jnp.where(odd, far, near)


def lon_difference(value):
    return pltpu.roll(value, LANES - 1, 1) - pltpu.roll(value, 1, 1)


def advance(states, row_pulls):
    north_pull, south_pull = row_pulls
    for step in range(STEPS):
        first, last = 1 + 2 * step, 3 * ROWS - 2 - 2 * step
        for state, depth in states:
            h, e, n = (state.at[field] for field in range(3))
            for row in range(first, last + 1):
                divergence = lon_difference(e[row]) + (n[row + 1] - n[row - 1])
                h[row] = h[row] - depth[row] * divergence
        for state, depth in states:
            h, e, n = (state.at[field] for field in range(3))
            for row in range(first + 1, last):
                row_pull = north_pull if row < ROWS else south_pull if row >= 2 * ROWS else PULL
                east, north = e[row], n[row]
                e[row] = east - PULL * lon_difference(h[row]) + ROTATION * north
                n[row] = north - row_pull * (h[row + 1] - h[row - 1]) - ROTATION * east


def inner_kernel(own_ref, near_ref, far_ref, out_ref, state, depth):
    def around(at):
        north, south = by_side(near_ref[at, :], far_ref[at, :])
        return enumerate((north, own_ref[at, :], south))

    for row in range(ROWS):
        for block, value in around(pl.ds((row * PER_ROW + SMALL) * 8 + 3, 1)):
            depth[ROWS * block + row] = PULL * jnp.broadcast_to(value, (8, LANES))
    row_pulls = pulls()

    def pair(which, carry):
        for half in range(2):
            tile = 2 * which + half
            for field in range(3):
                for row in range(ROWS):
                    at = pl.multiple_of((row * PER_ROW + MAIN + TILES * field + tile) * 8, 8)
                    for block, value in around(pl.ds(at, 8)):
                        state[half, field, ROWS * block + row] = value
        advance([(state.at[half], depth) for half in range(2)], row_pulls)
        for half in range(2):
            tile = 2 * which + half
            for field in range(3):
                for row in range(ROWS):
                    at = pl.multiple_of(((field * ROWS + row) * TILES + tile) * 8, 8)
                    out_ref[pl.ds(at, 8), :] = state[half, field, ROWS + row]
        return carry

    lax.fori_loop(0, TILES // 2, pair, 0)


def side_kernel(
    own_ref, near_ref, far_ref, halo_ref, near_halo_ref, far_halo_ref, inner_ref, weight_ref,
    split_ref, mean_out_ref, gram_ref, state, depth, heights, scaled,
):
    lane = lane_iota()
    low_lanes = (lane & 16) == 0
    sub = lax.broadcasted_iota(jnp.int32, (8, LANES), 0)

    def around(own, near, far, at):
        north, south = by_side(near[at, :], far[at, :])
        return north, own[at, :], south

    for row in range(ROWS):
        smalls = around(own_ref, near_ref, far_ref, block_at(row, SMALL))
        for which in range(4):
            sides = around(own_ref, near_ref, far_ref, block_at(row, SIDE + which))
            halos = around(halo_ref, near_halo_ref, far_halo_ref, pl.ds(((row // 2) * 4 + which) * 8, 8))
            for block, (small, side, halo) in enumerate(zip(smalls, sides, halos)):
                at = ROWS * block + row
                if MOVES[row % 4]:
                    halo = pltpu.roll(halo, LANES - MOVES[row % 4], 1)
                right = jnp.where(low_lanes, side, halo)
                left = jnp.where(low_lanes, halo, side)
                if which < 3:
                    state[0, which, at] = right
                    state[1, which, at] = left
                    continue
                for field in range(3):
                    state[2, field, at] = jnp.where(
                        sub == 0,
                        jnp.broadcast_to(small[field : field + 1, :], (8, LANES)),
                        jnp.where(
                            sub == 1,
                            jnp.broadcast_to(right[field : field + 1, :], (8, LANES)),
                            jnp.broadcast_to(left[field : field + 1, :], (8, LANES)),
                        ),
                    )
                of_right = PULL * jnp.broadcast_to(right[3:4, :], (8, LANES))
                of_left = PULL * jnp.broadcast_to(left[3:4, :], (8, LANES))
                whole = PULL * jnp.broadcast_to(small[3:4, :], (8, LANES))
                depth[0, at] = of_right
                depth[1, at] = of_left
                depth[2, at] = jnp.where(sub == 0, whole, jnp.where(sub == 1, of_right, of_left))
    advance([(state.at[which], depth.at[which]) for which in range(3)], pulls())

    from_right = (lane & 16) == 0
    edge = (lane < HALO) | (lane >= LANES - HALO)
    for field in range(3):
        for row in range(ROWS):
            plane = field * ROWS + row
            cols = slice(plane * LANES, (plane + 1) * LANES)
            sides = jnp.where(from_right, state[0, field, ROWS + row], state[1, field, ROWS + row])
            full = jnp.concatenate(
                [
                    jnp.where(
                        edge,
                        pltpu.roll(sides, (LANES - 16 - GROUP * tile) % LANES, 1),
                        inner_ref[pl.ds((plane * TILES + tile) * 8, 8), :],
                    )
                    for tile in range(TILES)
                ],
                0,
            )
            high = full.astype(jnp.bfloat16)
            rest = full - high.astype(jnp.float32)
            middle = rest.astype(jnp.bfloat16)
            split_ref[0:RANK, cols] = high
            split_ref[RANK : 2 * RANK, cols] = middle
            split_ref[2 * RANK : 3 * RANK, cols] = (rest - middle.astype(jnp.float32)).astype(jnp.bfloat16)
            mine = state[2, field, ROWS + row]
            both = jnp.where(from_right[0:1], mine[1:2, :], mine[2:3, :])
            mean = jnp.where(edge[0:1], pltpu.roll(both, LANES - 16, 1), mine[0:1, :])
            mean_out_ref[plane : plane + 1, :] = mean
            if field == 0:
                square = weight_ref[row : row + 1, :]
                heights[:, cols] = full
                scaled[0:RANK, cols] = full * square
                pulled = weight_ref[ROWS + row : ROWS + row + 1, :] - square * mean
                scaled[RANK : RANK + 8, cols] = jnp.broadcast_to(pulled, (8, LANES))
    gram = lax.dot_general(
        heights[...], scaled[...], NT, precision=HIGHEST, preferred_element_type=jnp.float32
    )
    gram = jnp.concatenate([gram, jnp.zeros((RANK, LANES - RANK - 8), jnp.float32)], 1)
    acc = None
    for tile in range(TILES):
        part = gram[8 * tile : 8 * tile + 8, :]
        if tile < 2:
            far = gram[8 * tile + 16 : 8 * tile + 24, :]
            part = jnp.where(lane == 31, pltpu.roll(part, LANES - 1, 1), part)
            part = jnp.where(lane == 30, pltpu.roll(far, LANES - 2, 1), part)
        moved = pltpu.roll(part, 32 * tile, 1) if tile else part
        acc = moved if acc is None else jnp.where(lane // 32 == tile, moved, acc)
    gram_ref[...] = acc


def analysis_kernel(parts_ref, split_ref, mean_ref, update_ref, factor_ref):
    lane = lane_iota()
    total = jnp.sum(parts_ref[...], 0)
    tiles, drives = [], [None] * TILES
    for tile in range(TILES):
        part = pltpu.roll(total, LANES - 32 * tile, 1) if tile else total
        if tile < 2:
            drives[tile] = pltpu.roll(part, 2 * RANK - 31, 1)
            drives[tile + 2] = pltpu.roll(part, 2 * RANK - 30, 1)
        tiles.append(part)
    lower = jnp.concatenate(tiles, 0)
    wide = lax.broadcasted_iota(jnp.int32, (RANK, LANES), 1)
    deep = lax.broadcasted_iota(jnp.int32, (RANK, LANES), 0)
    mirrored = jnp.concatenate([lower, jnp.zeros((LANES - RANK, LANES), jnp.float32)], 0).T[0:RANK, :]
    work = jnp.where(wide > deep, mirrored, lower)
    work = jnp.where(wide < RANK, work, 0.0) + jnp.where((wide == deep) | (wide == deep + RANK), 1.0, 0.0)
    work = jnp.where(wide == 2 * RANK, jnp.concatenate(drives, 0), work)
    for first in range(0, RANK, WIDTH):
        columns = [jnp.broadcast_to(work[:, k : k + 1], (RANK, LANES)) for k in range(first, first + WIDTH)]
        rows = [work[k : k + 1, :] for k in range(first, first + WIDTH)]
        for j in range(WIDTH):
            k = first + j
            inverse = 1.0 / columns[j][k : k + 1, :]
            scaled_row = rows[j] * inverse
            for i in range(j + 1, WIDTH):
                ratio = columns[j][first + i : first + i + 1, :] * inverse
                rows[i] = rows[i] - ratio * rows[j]
                columns[i] = columns[i] - columns[j] * ratio
            work = work - jnp.where(deep > k, columns[j], 0.0) * scaled_row
    pivots = jnp.sum(jnp.where(wide == deep, work, 0.0), 1, keepdims=True)
    work = work * lax.rsqrt(pivots)
    shift = jnp.sum(work * work[:, 2 * RANK : 2 * RANK + 1], 0, keepdims=True)
    mixed = jnp.concatenate([work, jnp.broadcast_to(shift, (8, LANES))], 0)[:, RANK : 2 * RANK]
    high = mixed.astype(jnp.bfloat16)
    rest = mixed - high.astype(jnp.float32)
    middle = rest.astype(jnp.bfloat16)
    low = (rest - middle.astype(jnp.float32)).astype(jnp.bfloat16)
    left = jnp.concatenate([high, high, high, middle, middle, low], 1)
    split = split_ref[...]
    fine = jnp.concatenate([split, split[0 : 2 * RANK], split[0:RANK]], 0)
    out = jnp.dot(left, fine, preferred_element_type=jnp.float32)
    for plane in range(PLANES):
        cols = slice(plane * LANES, (plane + 1) * LANES)
        for tile in range(TILES):
            factor_ref[pl.ds(8 * tile * PLANES + plane, 8, stride=PLANES), :] = out[8 * tile : 8 * tile + 8, cols]
        update_ref[plane : plane + 1, :] = mean_ref[plane : plane + 1, :] + out[RANK : RANK + 1, cols]


VMEM = pl.BlockSpec(memory_space=pltpu.VMEM)
SMALL_VMEM = pltpu.CompilerParams(vmem_limit_bytes=8 << 20)


def f32(*shape):
    return jax.ShapeDtypeStruct(shape, jnp.float32)


def chip(*shape):
    return pltpu.VMEM(shape, jnp.float32)


def on_chip(value):
    return pltpu.with_memory_space_constraint(value, pltpu.VMEM)


def swapped(value, axis, offset, periodic):
    count = lax.axis_size(axis)
    pairs = [(i, i + 1) for i in range(offset, count - 1, 2)]
    if offset and periodic:
        pairs.append((count - 1, 0))
    return lax.ppermute(value, axis, pairs + [(j, i) for i, j in pairs])


def sum_over(value, axis):
    count = lax.axis_size(axis)
    sent = jnp.broadcast_to(value[None], (count, *value.shape))
    return lax.all_to_all(sent, axis, 0, 0)


def per_device(
    background_expectation, factor, average_thickness, obs_cells, obs_count, obs_values, obs_error
):
    assert factor.shape == (RANK, 3, ROWS, LANES)
    slots = obs_cells.shape[0]
    block, even_edges, odd_edges, weights = pl.pallas_call(
        pack_kernel,
        out_shape=(chip(ROWS * PER_ROW * 8, LANES),) + (chip(ROWS * 8, LANES),) * 2 + (chip(2 * ROWS, LANES),),
        in_specs=[VMEM] * 7,
        out_specs=(VMEM,) * 4,
        name="pack",
    )(
        factor.reshape(RANK * PLANES, LANES), background_expectation.reshape(PLANES, LANES), average_thickness,
        obs_count.reshape(1, 1), obs_cells.reshape(1, slots), obs_values.reshape(1, slots), obs_error.reshape(1, slots),
    )
    block = on_chip(block)
    even_edges = swapped(even_edges, "lon", 0, True)
    odd_edges = swapped(odd_edges, "lon", 1, True)
    far = on_chip(swapped(block, "lat", 1, False))
    near = on_chip(swapped(block, "lat", 0, False))
    shape = (ROWS // 4, 4 * 8, LANES)
    eastern = (lax.broadcasted_iota(jnp.int32, shape, 2) & 8) // 8 != 1
    from_even = eastern == (lax.rem(lax.axis_index("lon"), 2) == 0)
    even_edges, odd_edges = even_edges.reshape(shape), odd_edges.reshape(shape)
    halo = jnp.stack(
        [jnp.where(from_even, even_edges, odd_edges), jnp.where(from_even, odd_edges, even_edges)], 1
    ).reshape(ROWS * 16, LANES)
    far_halo = on_chip(swapped(halo, "lat", 1, False))
    near_halo = on_chip(swapped(halo, "lat", 0, False))
    inner = pl.pallas_call(
        inner_kernel,
        out_shape=chip(RANK * PLANES, LANES),
        in_specs=[VMEM] * 3,
        out_specs=VMEM,
        scratch_shapes=[
            pltpu.VMEM((2, 3, 3 * ROWS, 8, LANES), jnp.float32),
            pltpu.VMEM((3 * ROWS, 8, LANES), jnp.float32),
        ],
        name="inner", compiler_params=SMALL_VMEM,
    )(block, near, far)
    split, mean, gram = pl.pallas_call(
        side_kernel,
        out_shape=(
            pltpu.VMEM((3 * RANK, PLANES * LANES), jnp.bfloat16),
            chip(PLANES, LANES),
            chip(8, LANES),
        ),
        in_specs=[VMEM] * 8,
        out_specs=(VMEM,) * 3,
        scratch_shapes=[
            pltpu.VMEM((3, 3, 3 * ROWS, 8, LANES), jnp.float32),
            pltpu.VMEM((3, 3 * ROWS, 8, LANES), jnp.float32),
            pltpu.VMEM((RANK, ROWS * LANES), jnp.float32),
            pltpu.VMEM((RANK + 8, ROWS * LANES), jnp.float32),
        ],
        name="side", compiler_params=SMALL_VMEM,
    )(block, near, far, on_chip(halo), near_halo, far_halo, on_chip(inner), on_chip(weights))
    gram = jnp.sum(sum_over(gram, "lat"), 0)
    parts = sum_over(gram, "lon")
    update, analysis = pl.pallas_call(
        analysis_kernel,
        out_shape=(f32(PLANES, LANES), f32(RANK * PLANES, LANES)),
        in_specs=[VMEM] * 3,
        out_specs=(VMEM, VMEM),
        name="analysis", compiler_params=SMALL_VMEM,
    )(on_chip(parts), on_chip(split), on_chip(mean))
    return update.reshape(background_expectation.shape), analysis.reshape(factor.shape)


def solution(mesh):
    return jax.shard_map(
        per_device,
        mesh=mesh,
        in_specs=(
            P(None, "lat", "lon"),
            P(None, None, "lat", "lon"),
            P("lat", "lon"),
            P(("lat", "lon")),
            P(("lat", "lon")),
            P(("lat", "lon")),
            P(("lat", "lon")),
        ),
        out_specs=(P(None, "lat", "lon"), P(None, None, "lat", "lon")),
        check_vma=False,
    )
```

```python
import jax
import jax.numpy as jnp
from jax import lax
from jax.experimental import pallas as pl
from jax.experimental.pallas import tpu as pltpu
from jax.sharding import PartitionSpec as P


STEPS = 4
TIME_STEP = 0.9
ROTATION = 0.25

RANK = 32
ROWS = 8
LANES = 128
HALO = 2 * STEPS
TILES = RANK // 8
PLANES = 3 * ROWS
GROUP = LANES // TILES
MAIN, SMALL = 0, 12
PER_ROW = 13
MOVES = (0, 16, 8, 24)
PULL = 0.5 * TIME_STEP
WIDTH = 8
HIGHEST = lax.Precision.HIGHEST
NT = (((1,), (1,)), ((), ()))


def lane_iota():
    return lax.broadcasted_iota(jnp.int32, (8, LANES), 1)


def member_rows(field, row, tile):
    return pl.ds(8 * tile * PLANES + field * ROWS + row, 8, stride=PLANES)


def block_at(row, tile):
    return pl.ds((row * PER_ROW + tile) * 8, 8)


def observed(count_ref, cells_ref, values_ref, error_ref):
    slots = cells_ref.shape[1]
    live = lax.broadcasted_iota(jnp.int32, (1, slots), 1) < count_ref[...]
    weight = jnp.where(live, 1.0, 0.0) / error_ref[...]
    square = weight * weight
    cells = cells_ref[...]
    row_of = cells // LANES
    lane_of = cells - row_of * LANES
    in_row = lax.broadcasted_iota(jnp.int32, (ROWS, slots), 0) == row_of
    spread = jnp.concatenate(
        [jnp.where(in_row, square, 0.0), jnp.where(in_row, square * values_ref[...], 0.0)], 0
    )
    in_lane = lax.broadcasted_iota(jnp.int32, (LANES, slots), 0) == lane_of
    return lax.dot_general(
        spread, jnp.where(in_lane, 1.0, 0.0), NT, precision=HIGHEST, preferred_element_type=jnp.float32
    )


def side_tile(values):
    part = lane_iota() // GROUP
    if len(values) == 1:
        side = pltpu.roll(values[0], 16, 1)
        side = jnp.where(part == 0, side, pltpu.roll(side, GROUP, 1))
        return jnp.where(part < 2, side, pltpu.roll(side, 2 * GROUP, 1))
    side = None
    for tile, value in enumerate(values):
        moved = pltpu.roll(value, 16 + GROUP * tile, 1)
        side = moved if side is None else jnp.where(part == tile, moved, side)
    return side


def pack_kernel(
    factor_ref, mean_ref, depth_ref, count_ref, cells_ref, values_ref, error_ref,
    block_ref, side_ref, even_edge_ref, odd_edge_ref, weight_ref,
):
    lane = lane_iota()
    octet = (lane // 8) & 3
    weight_ref[...] = observed(count_ref, cells_ref, values_ref, error_ref)
    even = lax.rem(lax.axis_index("lon"), 2) == 0
    eastward, westward = {}, {}
    for row in range(ROWS):
        small = jnp.concatenate(
            [mean_ref[f * ROWS + row : f * ROWS + row + 1, :] for f in range(3)]
            + [depth_ref[row : row + 1, :]] * 5,
            0,
        )
        block_ref[block_at(row, SMALL), :] = small
        sides = []
        for field in range(3):
            values = [factor_ref[member_rows(field, row, tile), :] for tile in range(TILES)]
            for tile, value in enumerate(values):
                block_ref[block_at(row, MAIN + TILES * field + tile), :] = value
            sides.append(side_tile(values))
        sides.append(side_tile([small]))
        for which, side in enumerate(sides):
            side_ref[pl.ds((row * 4 + which) * 8, 8), :] = side
            move = MOVES[row % 4]
            moved = pltpu.roll(side, move, 1) if move else side
            if row % 4 == 0:
                eastward[which] = westward[which] = moved
                continue
            eastward[which] = jnp.where(octet == (1 + move // 8) % 4, moved, eastward[which])
            westward[which] = jnp.where(octet == (2 + move // 8) % 4, moved, westward[which])
            if row % 4 == 3:
                at = pl.ds(((row // 4) * 4 + which) * 8, 8)
                even_edge_ref[at, :] = jnp.where(even, eastward[which], westward[which])
                odd_edge_ref[at, :] = jnp.where(even, westward[which], eastward[which])


def pulls():
    band = lax.axis_index("lat")
    bands = lax.axis_size("lat")
    north = jnp.where(band > 0, PULL, 0.0)
    south = jnp.where(band < bands - 1, PULL, 0.0)
    return north, south


def by_side(near, far):
    odd = lax.rem(lax.axis_index("lat"), 2) == 1
    return jnp.where(odd, near, far), jnp.where(odd, far, near)


def lon_difference(value):
    return pltpu.roll(value, LANES - 1, 1) - pltpu.roll(value, 1, 1)


def advance(states, row_pulls):
    north_pull, south_pull = row_pulls
    for step in range(STEPS):
        first, last = 1 + 2 * step, 3 * ROWS - 2 - 2 * step
        for state, depth in states:
            h, e, n = (state.at[field] for field in range(3))
            for row in range(first, last + 1):
                divergence = lon_difference(e[row]) + (n[row + 1] - n[row - 1])
                h[row] = h[row] - depth[row] * divergence
        for state, depth in states:
            h, e, n = (state.at[field] for field in range(3))
            for row in range(first + 1, last):
                row_pull = north_pull if row < ROWS else south_pull if row >= 2 * ROWS else PULL
                east, north = e[row], n[row]
                e[row] = east - PULL * lon_difference(h[row]) + ROTATION * north
                n[row] = north - row_pull * (h[row + 1] - h[row - 1]) - ROTATION * east


def inner_kernel(own_ref, near_ref, far_ref, out_ref, state, depth):
    def around(at):
        north, south = by_side(near_ref[at, :], far_ref[at, :])
        return enumerate((north, own_ref[at, :], south))

    for row in range(ROWS):
        for block, value in around(pl.ds((row * PER_ROW + SMALL) * 8 + 3, 1)):
            depth[ROWS * block + row] = PULL * jnp.broadcast_to(value, (8, LANES))
    row_pulls = pulls()

    def pair(which, carry):
        for half in range(2):
            tile = 2 * which + half
            for field in range(3):
                for row in range(ROWS):
                    at = pl.multiple_of((row * PER_ROW + MAIN + TILES * field + tile) * 8, 8)
                    for block, value in around(pl.ds(at, 8)):
                        state[half, field, ROWS * block + row] = value
        advance([(state.at[half], depth) for half in range(2)], row_pulls)
        for half in range(2):
            tile = 2 * which + half
            for field in range(3):
                for row in range(ROWS):
                    at = pl.multiple_of(((field * ROWS + row) * TILES + tile) * 8, 8)
                    out_ref[pl.ds(at, 8), :] = state[half, field, ROWS + row]
        return carry

    lax.fori_loop(0, TILES // 2, pair, 0)


def side_kernel(
    own_ref, side_ref, near_ref, far_ref, halo_ref, near_halo_ref, far_halo_ref, inner_ref, weight_ref,
    split_ref, mean_out_ref, gram_ref, state, depth, heights, scaled,
):
    lane = lane_iota()
    low_lanes = (lane & 16) == 0
    sub = lax.broadcasted_iota(jnp.int32, (8, LANES), 0)

    def around(own, near, far, at):
        north, south = by_side(near[at, :], far[at, :])
        return north, own[at, :], south

    for row in range(ROWS):
        smalls = around(own_ref, near_ref, far_ref, block_at(row, SMALL))
        for which in range(4):
            tiles = [SMALL] if which == 3 else range(TILES * which, TILES * (which + 1))
            pairs = [by_side(near_ref[block_at(row, t), :], far_ref[block_at(row, t), :]) for t in tiles]
            north, south = (side_tile(values) for values in zip(*pairs))
            sides = (north, side_ref[pl.ds((row * 4 + which) * 8, 8), :], south)
            halos = around(halo_ref, near_halo_ref, far_halo_ref, pl.ds(((row // 2) * 4 + which) * 8, 8))
            for block, (small, side, halo) in enumerate(zip(smalls, sides, halos)):
                at = ROWS * block + row
                if MOVES[row % 4]:
                    halo = pltpu.roll(halo, LANES - MOVES[row % 4], 1)
                right = jnp.where(low_lanes, side, halo)
                left = jnp.where(low_lanes, halo, side)
                if which < 3:
                    state[0, which, at] = right
                    state[1, which, at] = left
                    continue
                for field in range(3):
                    state[2, field, at] = jnp.where(
                        sub == 0,
                        jnp.broadcast_to(small[field : field + 1, :], (8, LANES)),
                        jnp.where(
                            sub == 1,
                            jnp.broadcast_to(right[field : field + 1, :], (8, LANES)),
                            jnp.broadcast_to(left[field : field + 1, :], (8, LANES)),
                        ),
                    )
                of_right = PULL * jnp.broadcast_to(right[3:4, :], (8, LANES))
                of_left = PULL * jnp.broadcast_to(left[3:4, :], (8, LANES))
                whole = PULL * jnp.broadcast_to(small[3:4, :], (8, LANES))
                depth[0, at] = of_right
                depth[1, at] = of_left
                depth[2, at] = jnp.where(sub == 0, whole, jnp.where(sub == 1, of_right, of_left))
    advance([(state.at[which], depth.at[which]) for which in range(3)], pulls())

    from_right = (lane & 16) == 0
    edge = (lane < HALO) | (lane >= LANES - HALO)
    for field in range(3):
        for row in range(ROWS):
            plane = field * ROWS + row
            cols = slice(plane * LANES, (plane + 1) * LANES)
            sides = jnp.where(from_right, state[0, field, ROWS + row], state[1, field, ROWS + row])
            full = jnp.concatenate(
                [
                    jnp.where(
                        edge,
                        pltpu.roll(sides, (LANES - 16 - GROUP * tile) % LANES, 1),
                        inner_ref[pl.ds((plane * TILES + tile) * 8, 8), :],
                    )
                    for tile in range(TILES)
                ],
                0,
            )
            high = full.astype(jnp.bfloat16)
            rest = full - high.astype(jnp.float32)
            middle = rest.astype(jnp.bfloat16)
            split_ref[0:RANK, cols] = high
            split_ref[RANK : 2 * RANK, cols] = middle
            split_ref[2 * RANK : 3 * RANK, cols] = (rest - middle.astype(jnp.float32)).astype(jnp.bfloat16)
            mine = state[2, field, ROWS + row]
            both = jnp.where(from_right[0:1], mine[1:2, :], mine[2:3, :])
            mean = jnp.where(edge[0:1], pltpu.roll(both, LANES - 16, 1), mine[0:1, :])
            mean_out_ref[plane : plane + 1, :] = mean
            if field == 0:
                square = weight_ref[row : row + 1, :]
                heights[:, cols] = full
                scaled[0:RANK, cols] = full * square
                pulled = weight_ref[ROWS + row : ROWS + row + 1, :] - square * mean
                scaled[RANK : RANK + 8, cols] = jnp.broadcast_to(pulled, (8, LANES))
    gram = lax.dot_general(
        heights[...], scaled[...], NT, precision=HIGHEST, preferred_element_type=jnp.float32
    )
    gram = jnp.concatenate([gram, jnp.zeros((RANK, LANES - RANK - 8), jnp.float32)], 1)
    acc = None
    for tile in range(TILES):
        part = gram[8 * tile : 8 * tile + 8, :]
        if tile < 2:
            far = gram[8 * tile + 16 : 8 * tile + 24, :]
            part = jnp.where(lane == 31, pltpu.roll(part, LANES - 1, 1), part)
            part = jnp.where(lane == 30, pltpu.roll(far, LANES - 2, 1), part)
        moved = pltpu.roll(part, 32 * tile, 1) if tile else part
        acc = moved if acc is None else jnp.where(lane // 32 == tile, moved, acc)
    gram_ref[...] = acc


def analysis_kernel(parts_ref, split_ref, mean_ref, update_ref, factor_ref):
    lane = lane_iota()
    total = jnp.sum(parts_ref[...], 0)
    tiles, drives = [], [None] * TILES
    for tile in range(TILES):
        part = pltpu.roll(total, LANES - 32 * tile, 1) if tile else total
        if tile < 2:
            drives[tile] = pltpu.roll(part, 2 * RANK - 31, 1)
            drives[tile + 2] = pltpu.roll(part, 2 * RANK - 30, 1)
        tiles.append(part)
    lower = jnp.concatenate(tiles, 0)
    wide = lax.broadcasted_iota(jnp.int32, (RANK, LANES), 1)
    deep = lax.broadcasted_iota(jnp.int32, (RANK, LANES), 0)
    mirrored = jnp.concatenate([lower, jnp.zeros((LANES - RANK, LANES), jnp.float32)], 0).T[0:RANK, :]
    work = jnp.where(wide > deep, mirrored, lower)
    work = jnp.where(wide < RANK, work, 0.0) + jnp.where((wide == deep) | (wide == deep + RANK), 1.0, 0.0)
    work = jnp.where(wide == 2 * RANK, jnp.concatenate(drives, 0), work)
    for first in range(0, RANK, WIDTH):
        columns = [jnp.broadcast_to(work[:, k : k + 1], (RANK, LANES)) for k in range(first, first + WIDTH)]
        rows = [work[k : k + 1, :] for k in range(first, first + WIDTH)]
        for j in range(WIDTH):
            k = first + j
            inverse = 1.0 / columns[j][k : k + 1, :]
            scaled_row = rows[j] * inverse
            for i in range(j + 1, WIDTH):
                ratio = columns[j][first + i : first + i + 1, :] * inverse
                rows[i] = rows[i] - ratio * rows[j]
                columns[i] = columns[i] - columns[j] * ratio
            work = work - jnp.where(deep > k, columns[j], 0.0) * scaled_row
    pivots = jnp.sum(jnp.where(wide == deep, work, 0.0), 1, keepdims=True)
    work = work * lax.rsqrt(pivots)
    shift = jnp.sum(work * work[:, 2 * RANK : 2 * RANK + 1], 0, keepdims=True)
    mixed = jnp.concatenate([work, jnp.broadcast_to(shift, (8, LANES))], 0)[:, RANK : 2 * RANK]
    high = mixed.astype(jnp.bfloat16)
    rest = mixed - high.astype(jnp.float32)
    middle = rest.astype(jnp.bfloat16)
    low = (rest - middle.astype(jnp.float32)).astype(jnp.bfloat16)
    left = jnp.concatenate([high, high, high, middle, middle, low], 1)
    split = split_ref[...]
    fine = jnp.concatenate([split, split[0 : 2 * RANK], split[0:RANK]], 0)
    out = jnp.dot(left, fine, preferred_element_type=jnp.float32)
    for plane in range(PLANES):
        cols = slice(plane * LANES, (plane + 1) * LANES)
        for tile in range(TILES):
            factor_ref[pl.ds(8 * tile * PLANES + plane, 8, stride=PLANES), :] = out[8 * tile : 8 * tile + 8, cols]
        update_ref[plane : plane + 1, :] = mean_ref[plane : plane + 1, :] + out[RANK : RANK + 1, cols]


VMEM = pl.BlockSpec(memory_space=pltpu.VMEM)
SMALL_VMEM = pltpu.CompilerParams(vmem_limit_bytes=8 << 20)


def f32(*shape):
    return jax.ShapeDtypeStruct(shape, jnp.float32)


def chip(*shape):
    return pltpu.VMEM(shape, jnp.float32)


def on_chip(value):
    return pltpu.with_memory_space_constraint(value, pltpu.VMEM)


def swapped(value, axis, offset, periodic):
    count = lax.axis_size(axis)
    pairs = [(i, i + 1) for i in range(offset, count - 1, 2)]
    if offset and periodic:
        pairs.append((count - 1, 0))
    return lax.ppermute(value, axis, pairs + [(j, i) for i, j in pairs])


def sum_over(value, axis):
    count = lax.axis_size(axis)
    sent = jnp.broadcast_to(value[None], (count, *value.shape))
    return lax.all_to_all(sent, axis, 0, 0)


def per_device(
    background_expectation, factor, average_thickness, obs_cells, obs_count, obs_values, obs_error
):
    assert factor.shape == (RANK, 3, ROWS, LANES)
    slots = obs_cells.shape[0]
    block, sides, even_edges, odd_edges, weights = pl.pallas_call(
        pack_kernel,
        out_shape=(
            chip(ROWS * PER_ROW * 8, LANES),
            chip(ROWS * 4 * 8, LANES),
            chip(ROWS * 8, LANES),
            chip(ROWS * 8, LANES),
            chip(2 * ROWS, LANES),
        ),
        in_specs=[VMEM] * 7,
        out_specs=(VMEM,) * 5,
        name="pack",
    )(
        factor.reshape(RANK * PLANES, LANES), background_expectation.reshape(PLANES, LANES), average_thickness,
        obs_count.reshape(1, 1), obs_cells.reshape(1, slots), obs_values.reshape(1, slots), obs_error.reshape(1, slots),
    )
    block = on_chip(block)
    even_edges = swapped(even_edges, "lon", 0, True)
    odd_edges = swapped(odd_edges, "lon", 1, True)
    far = on_chip(swapped(block, "lat", 1, False))
    near = on_chip(swapped(block, "lat", 0, False))
    shape = (ROWS // 4, 4 * 8, LANES)
    eastern = (lax.broadcasted_iota(jnp.int32, shape, 2) & 8) // 8 != 1
    from_even = eastern == (lax.rem(lax.axis_index("lon"), 2) == 0)
    even_edges, odd_edges = even_edges.reshape(shape), odd_edges.reshape(shape)
    halo = jnp.stack(
        [jnp.where(from_even, even_edges, odd_edges), jnp.where(from_even, odd_edges, even_edges)], 1
    ).reshape(ROWS * 16, LANES)
    far_halo = on_chip(swapped(halo, "lat", 1, False))
    near_halo = on_chip(swapped(halo, "lat", 0, False))
    inner = pl.pallas_call(
        inner_kernel,
        out_shape=chip(RANK * PLANES, LANES),
        in_specs=[VMEM] * 3,
        out_specs=VMEM,
        scratch_shapes=[
            pltpu.VMEM((2, 3, 3 * ROWS, 8, LANES), jnp.float32),
            pltpu.VMEM((3 * ROWS, 8, LANES), jnp.float32),
        ],
        name="inner", compiler_params=SMALL_VMEM,
    )(block, near, far)
    split, mean, gram = pl.pallas_call(
        side_kernel,
        out_shape=(
            pltpu.VMEM((3 * RANK, PLANES * LANES), jnp.bfloat16),
            chip(PLANES, LANES),
            chip(8, LANES),
        ),
        in_specs=[VMEM] * 9,
        out_specs=(VMEM,) * 3,
        scratch_shapes=[
            pltpu.VMEM((3, 3, 3 * ROWS, 8, LANES), jnp.float32),
            pltpu.VMEM((3, 3 * ROWS, 8, LANES), jnp.float32),
            pltpu.VMEM((RANK, ROWS * LANES), jnp.float32),
            pltpu.VMEM((RANK + 8, ROWS * LANES), jnp.float32),
        ],
        name="side", compiler_params=SMALL_VMEM,
    )(block, on_chip(sides), near, far, on_chip(halo), near_halo, far_halo, on_chip(inner), on_chip(weights))
    gram = jnp.sum(sum_over(gram, "lat"), 0)
    parts = sum_over(gram, "lon")
    update, analysis = pl.pallas_call(
        analysis_kernel,
        out_shape=(f32(PLANES, LANES), f32(RANK * PLANES, LANES)),
        in_specs=[VMEM] * 3,
        out_specs=(VMEM, VMEM),
        name="analysis", compiler_params=SMALL_VMEM,
    )(on_chip(parts), on_chip(split), on_chip(mean))
    return update.reshape(background_expectation.shape), analysis.reshape(factor.shape)


def solution(mesh):
    return jax.shard_map(
        per_device,
        mesh=mesh,
        in_specs=(
            P(None, "lat", "lon"),
            P(None, None, "lat", "lon"),
            P("lat", "lon"),
            P(("lat", "lon")),
            P(("lat", "lon")),
            P(("lat", "lon")),
            P(("lat", "lon")),
        ),
        out_specs=(P(None, "lat", "lon"), P(None, None, "lat", "lon")),
        check_vma=False,
    )
```

```python
import jax
import jax.numpy as jnp
from jax import lax
from jax.experimental import pallas as pl
from jax.experimental.pallas import tpu as pltpu
from jax.sharding import PartitionSpec as P


STEPS = 4
TIME_STEP = 0.9
ROTATION = 0.25

RANK = 32
ROWS = 8
LANES = 128
HALO = 2 * STEPS
TILES = RANK // 8
PLANES = 3 * ROWS
GROUP = LANES // TILES
MAIN, SMALL, SIDE = 0, 12, 13
PER_ROW = 17
BLOCK = ROWS * PER_ROW * 8
MOVES = (0, 16, 8, 24)
PULL = 0.5 * TIME_STEP
WIDTH = 8
HIGHEST = lax.Precision.HIGHEST
NT = (((1,), (1,)), ((), ()))


def lane_iota():
    return lax.broadcasted_iota(jnp.int32, (8, LANES), 1)


def member_rows(field, row, tile):
    return pl.ds(8 * tile * PLANES + field * ROWS + row, 8, stride=PLANES)


def block_at(row, tile):
    return pl.ds((row * PER_ROW + tile) * 8, 8)


def weight_kernel(count_ref, cells_ref, values_ref, error_ref, out_ref):
    slots = cells_ref.shape[1]
    live = lax.broadcasted_iota(jnp.int32, (1, slots), 1) < count_ref[...]
    weight = jnp.where(live, 1.0, 0.0) / error_ref[...]
    square = weight * weight
    cells = cells_ref[...]
    row_of = cells // LANES
    lane_of = cells - row_of * LANES
    in_row = lax.broadcasted_iota(jnp.int32, (ROWS, slots), 0) == row_of
    spread = jnp.concatenate(
        [jnp.where(in_row, square, 0.0), jnp.where(in_row, square * values_ref[...], 0.0)], 0
    )
    in_lane = lax.broadcasted_iota(jnp.int32, (LANES, slots), 0) == lane_of
    out_ref[...] = lax.dot_general(
        spread, jnp.where(in_lane, 1.0, 0.0), NT, precision=HIGHEST, preferred_element_type=jnp.float32
    )


def pack_kernel(
    factor_ref, mean_ref, depth_ref, cells_ref, values_ref, error_ref,
    block_ref, near_block_ref, even_edge_ref, odd_edge_ref, cells_out_ref, values_out_ref, error_out_ref,
):
    lane = lane_iota()
    part = lane // GROUP
    octet = (lane // 8) & 3
    cells_out_ref[...] = cells_ref[...]
    values_out_ref[...] = values_ref[...]
    error_out_ref[...] = error_ref[...]

    def keep(row, tile, value):
        block_ref[block_at(row, tile), :] = value
        near_block_ref[block_at(row, tile), :] = value

    even = lax.rem(lax.axis_index("lon"), 2) == 0
    eastward, westward = {}, {}
    for row in range(ROWS):
        small = jnp.concatenate(
            [mean_ref[f * ROWS + row : f * ROWS + row + 1, :] for f in range(3)]
            + [depth_ref[row : row + 1, :]] * 5,
            0,
        )
        keep(row, SMALL, small)
        sides = []
        for field in range(3):
            side = None
            for tile in range(TILES):
                value = factor_ref[member_rows(field, row, tile), :]
                keep(row, MAIN + TILES * field + tile, value)
                moved = pltpu.roll(value, 16 + GROUP * tile, 1)
                side = moved if side is None else jnp.where(part == tile, moved, side)
            sides.append(side)
        side = pltpu.roll(small, 16, 1)
        side = jnp.where(part == 0, side, pltpu.roll(side, GROUP, 1))
        sides.append(jnp.where(part < 2, side, pltpu.roll(side, 2 * GROUP, 1)))
        for which, side in enumerate(sides):
            keep(row, SIDE + which, side)
            move = MOVES[row % 4]
            moved = pltpu.roll(side, move, 1) if move else side
            if row % 4 == 0:
                eastward[which] = westward[which] = moved
                continue
            eastward[which] = jnp.where(octet == (1 + move // 8) % 4, moved, eastward[which])
            westward[which] = jnp.where(octet == (2 + move // 8) % 4, moved, westward[which])
            if row % 4 == 3:
                at = pl.ds(((row // 4) * 4 + which) * 8, 8)
                even_edge_ref[at, :] = jnp.where(even, eastward[which], westward[which])
                odd_edge_ref[at, :] = jnp.where(even, westward[which], eastward[which])


def pulls():
    band = lax.axis_index("lat")
    bands = lax.axis_size("lat")
    north = jnp.where(band > 0, PULL, 0.0)
    south = jnp.where(band < bands - 1, PULL, 0.0)
    return north, south


def by_side(near, far):
    odd = lax.rem(lax.axis_index("lat"), 2) == 1
    return jnp.where(odd, near, far), jnp.where(odd, far, near)


def lon_difference(value):
    return pltpu.roll(value, LANES - 1, 1) - pltpu.roll(value, 1, 1)


def advance(states, row_pulls):
    north_pull, south_pull = row_pulls
    for step in range(STEPS):
        first, last = 1 + 2 * step, 3 * ROWS - 2 - 2 * step
        for state, depth in states:
            h, e, n = (state.at[field] for field in range(3))
            for row in range(first, last + 1):
                divergence = lon_difference(e[row]) + (n[row + 1] - n[row - 1])
                h[row] = h[row] - depth[row] * divergence
        for state, depth in states:
            h, e, n = (state.at[field] for field in range(3))
            for row in range(first + 1, last):
                row_pull = north_pull if row < ROWS else south_pull if row >= 2 * ROWS else PULL
                east, north = e[row], n[row]
                e[row] = east - PULL * lon_difference(h[row]) + ROTATION * north
                n[row] = north - row_pull * (h[row + 1] - h[row - 1]) - ROTATION * east


def inner_kernel(own_ref, near_ref, far_ref, out_ref, state, depth):
    def around(at):
        north, south = by_side(near_ref[at, :], far_ref[at, :])
        return enumerate((north, own_ref[at, :], south))

    for row in range(ROWS):
        for block, value in around(pl.ds((row * PER_ROW + SMALL) * 8 + 3, 1)):
            depth[ROWS * block + row] = PULL * jnp.broadcast_to(value, (8, LANES))
    row_pulls = pulls()

    def pair(which, carry):
        for half in range(2):
            tile = 2 * which + half
            for field in range(3):
                for row in range(ROWS):
                    at = pl.multiple_of((row * PER_ROW + MAIN + TILES * field + tile) * 8, 8)
                    for block, value in around(pl.ds(at, 8)):
                        state[half, field, ROWS * block + row] = value
        advance([(state.at[half], depth) for half in range(2)], row_pulls)
        for half in range(2):
            tile = 2 * which + half
            for field in range(3):
                for row in range(ROWS):
                    at = pl.multiple_of(((field * ROWS + row) * TILES + tile) * 8, 8)
                    out_ref[pl.ds(at, 8), :] = state[half, field, ROWS + row]
        return carry

    lax.fori_loop(0, TILES // 2, pair, 0)


def side_kernel(
    own_ref, near_ref, far_ref, halo_ref, far_halo_ref, inner_ref, weight_ref,
    split_ref, mean_out_ref, gram_ref, state, depth, heights, scaled,
):
    lane = lane_iota()
    low_lanes = (lane & 16) == 0
    sub = lax.broadcasted_iota(jnp.int32, (8, LANES), 0)

    def around(own, near, far, at, below=0):
        north, south = by_side(near[pl.ds(below + at.start, 8), :], far[at, :])
        return north, own[at, :], south

    for row in range(ROWS):
        smalls = around(own_ref, near_ref, far_ref, block_at(row, SMALL))
        for which in range(4):
            sides = around(own_ref, near_ref, far_ref, block_at(row, SIDE + which))
            halos = around(halo_ref, near_ref, far_halo_ref, pl.ds(((row // 2) * 4 + which) * 8, 8), BLOCK)
            for block, (small, side, halo) in enumerate(zip(smalls, sides, halos)):
                at = ROWS * block + row
                if MOVES[row % 4]:
                    halo = pltpu.roll(halo, LANES - MOVES[row % 4], 1)
                right = jnp.where(low_lanes, side, halo)
                left = jnp.where(low_lanes, halo, side)
                if which < 3:
                    state[0, which, at] = right
                    state[1, which, at] = left
                    continue
                for field in range(3):
                    state[2, field, at] = jnp.where(
                        sub == 0,
                        jnp.broadcast_to(small[field : field + 1, :], (8, LANES)),
                        jnp.where(
                            sub == 1,
                            jnp.broadcast_to(right[field : field + 1, :], (8, LANES)),
                            jnp.broadcast_to(left[field : field + 1, :], (8, LANES)),
                        ),
                    )
                of_right = PULL * jnp.broadcast_to(right[3:4, :], (8, LANES))
                of_left = PULL * jnp.broadcast_to(left[3:4, :], (8, LANES))
                whole = PULL * jnp.broadcast_to(small[3:4, :], (8, LANES))
                depth[0, at] = of_right
                depth[1, at] = of_left
                depth[2, at] = jnp.where(sub == 0, whole, jnp.where(sub == 1, of_right, of_left))
    advance([(state.at[which], depth.at[which]) for which in range(3)], pulls())

    from_right = (lane & 16) == 0
    edge = (lane < HALO) | (lane >= LANES - HALO)
    for field in range(3):
        for row in range(ROWS):
            plane = field * ROWS + row
            cols = slice(plane * LANES, (plane + 1) * LANES)
            sides = jnp.where(from_right, state[0, field, ROWS + row], state[1, field, ROWS + row])
            full = jnp.concatenate(
                [
                    jnp.where(
                        edge,
                        pltpu.roll(sides, (LANES - 16 - GROUP * tile) % LANES, 1),
                        inner_ref[pl.ds((plane * TILES + tile) * 8, 8), :],
                    )
                    for tile in range(TILES)
                ],
                0,
            )
            high = full.astype(jnp.bfloat16)
            rest = full - high.astype(jnp.float32)
            middle = rest.astype(jnp.bfloat16)
            split_ref[0:RANK, cols] = high
            split_ref[RANK : 2 * RANK, cols] = middle
            split_ref[2 * RANK : 3 * RANK, cols] = (rest - middle.astype(jnp.float32)).astype(jnp.bfloat16)
            mine = state[2, field, ROWS + row]
            both = jnp.where(from_right[0:1], mine[1:2, :], mine[2:3, :])
            mean = jnp.where(edge[0:1], pltpu.roll(both, LANES - 16, 1), mine[0:1, :])
            mean_out_ref[plane : plane + 1, :] = mean
            if field == 0:
                square = weight_ref[row : row + 1, :]
                heights[:, cols] = full
                scaled[0:RANK, cols] = full * square
                pulled = weight_ref[ROWS + row : ROWS + row + 1, :] - square * mean
                scaled[RANK : RANK + 8, cols] = jnp.broadcast_to(pulled, (8, LANES))
    gram = lax.dot_general(
        heights[...], scaled[...], NT, precision=HIGHEST, preferred_element_type=jnp.float32
    )
    gram = jnp.concatenate([gram, jnp.zeros((RANK, LANES - RANK - 8), jnp.float32)], 1)
    acc = None
    for tile in range(TILES):
        part = gram[8 * tile : 8 * tile + 8, :]
        if tile < 2:
            far = gram[8 * tile + 16 : 8 * tile + 24, :]
            part = jnp.where(lane == 31, pltpu.roll(part, LANES - 1, 1), part)
            part = jnp.where(lane == 30, pltpu.roll(far, LANES - 2, 1), part)
        moved = pltpu.roll(part, 32 * tile, 1) if tile else part
        acc = moved if acc is None else jnp.where(lane // 32 == tile, moved, acc)
    gram_ref[...] = acc


def analysis_kernel(parts_ref, split_ref, mean_ref, update_ref, factor_ref):
    lane = lane_iota()
    total = jnp.sum(parts_ref[...], 0)
    tiles, drives = [], [None] * TILES
    for tile in range(TILES):
        part = pltpu.roll(total, LANES - 32 * tile, 1) if tile else total
        if tile < 2:
            drives[tile] = pltpu.roll(part, 2 * RANK - 31, 1)
            drives[tile + 2] = pltpu.roll(part, 2 * RANK - 30, 1)
        tiles.append(part)
    lower = jnp.concatenate(tiles, 0)
    wide = lax.broadcasted_iota(jnp.int32, (RANK, LANES), 1)
    deep = lax.broadcasted_iota(jnp.int32, (RANK, LANES), 0)
    mirrored = jnp.concatenate([lower, jnp.zeros((LANES - RANK, LANES), jnp.float32)], 0).T[0:RANK, :]
    work = jnp.where(wide > deep, mirrored, lower)
    work = jnp.where(wide < RANK, work, 0.0) + jnp.where((wide == deep) | (wide == deep + RANK), 1.0, 0.0)
    work = jnp.where(wide == 2 * RANK, jnp.concatenate(drives, 0), work)
    for first in range(0, RANK, WIDTH):
        columns = [jnp.broadcast_to(work[:, k : k + 1], (RANK, LANES)) for k in range(first, first + WIDTH)]
        rows = [work[k : k + 1, :] for k in range(first, first + WIDTH)]
        for j in range(WIDTH):
            k = first + j
            inverse = 1.0 / columns[j][k : k + 1, :]
            scaled_row = rows[j] * inverse
            for i in range(j + 1, WIDTH):
                ratio = columns[j][first + i : first + i + 1, :] * inverse
                rows[i] = rows[i] - ratio * rows[j]
                columns[i] = columns[i] - columns[j] * ratio
            work = work - jnp.where(deep > k, columns[j], 0.0) * scaled_row
    pivots = jnp.sum(jnp.where(wide == deep, work, 0.0), 1, keepdims=True)
    work = work * lax.rsqrt(pivots)
    shift = jnp.sum(work * work[:, 2 * RANK : 2 * RANK + 1], 0, keepdims=True)
    mixed = jnp.concatenate([work, jnp.broadcast_to(shift, (8, LANES))], 0)[:, RANK : 2 * RANK]
    high = mixed.astype(jnp.bfloat16)
    rest = mixed - high.astype(jnp.float32)
    middle = rest.astype(jnp.bfloat16)
    low = (rest - middle.astype(jnp.float32)).astype(jnp.bfloat16)
    left = jnp.concatenate([high, high, high, middle, middle, low], 1)
    split = split_ref[...]
    fine = jnp.concatenate([split, split[0 : 2 * RANK], split[0:RANK]], 0)
    out = jnp.dot(left, fine, preferred_element_type=jnp.float32)
    for plane in range(PLANES):
        cols = slice(plane * LANES, (plane + 1) * LANES)
        for tile in range(TILES):
            factor_ref[pl.ds(8 * tile * PLANES + plane, 8, stride=PLANES), :] = out[8 * tile : 8 * tile + 8, cols]
        update_ref[plane : plane + 1, :] = mean_ref[plane : plane + 1, :] + out[RANK : RANK + 1, cols]


VMEM = pl.BlockSpec(memory_space=pltpu.VMEM)
SMALL_VMEM = pltpu.CompilerParams(vmem_limit_bytes=8 << 20)


def f32(*shape):
    return jax.ShapeDtypeStruct(shape, jnp.float32)


def chip(*shape):
    return pltpu.VMEM(shape, jnp.float32)


def on_chip(value):
    return pltpu.with_memory_space_constraint(value, pltpu.VMEM)


def swapped(value, axis, offset, periodic):
    count = lax.axis_size(axis)
    pairs = [(i, i + 1) for i in range(offset, count - 1, 2)]
    if offset and periodic:
        pairs.append((count - 1, 0))
    return lax.ppermute(value, axis, pairs + [(j, i) for i, j in pairs])


def sum_over(value, axis):
    count = lax.axis_size(axis)
    sent = jnp.broadcast_to(value[None], (count, *value.shape))
    return lax.all_to_all(sent, axis, 0, 0)


def per_device(
    background_expectation, factor, average_thickness, obs_cells, obs_count, obs_values, obs_error
):
    assert factor.shape == (RANK, 3, ROWS, LANES)
    slots = obs_cells.shape[0]
    block, near_block, even_edges, odd_edges, cells, values, error = pl.pallas_call(
        pack_kernel,
        out_shape=(
            chip(BLOCK, LANES),
            chip(BLOCK + ROWS * 16, LANES),
            chip(ROWS * 8, LANES),
            chip(ROWS * 8, LANES),
            pltpu.VMEM((1, slots), jnp.int32),
            chip(1, slots),
            chip(1, slots),
        ),
        in_specs=[VMEM] * 6,
        out_specs=(VMEM,) * 7,
        name="pack",
    )(
        factor.reshape(RANK * PLANES, LANES), background_expectation.reshape(PLANES, LANES), average_thickness,
        obs_cells.reshape(1, slots), obs_values.reshape(1, slots), obs_error.reshape(1, slots),
    )
    block = on_chip(block)
    odd_edges = swapped(odd_edges, "lon", 1, True)
    far = on_chip(swapped(block, "lat", 1, False))
    even_edges = swapped(even_edges, "lon", 0, True)
    weights = pl.pallas_call(
        weight_kernel, out_shape=chip(2 * ROWS, LANES), in_specs=[VMEM] * 4, out_specs=VMEM, name="weigh"
    )(obs_count.reshape(1, 1), on_chip(cells), on_chip(values), on_chip(error))
    shape = (ROWS // 4, 4 * 8, LANES)
    eastern = (lax.broadcasted_iota(jnp.int32, shape, 2) & 8) // 8 != 1
    from_even = eastern == (lax.rem(lax.axis_index("lon"), 2) == 0)
    even_edges, odd_edges = even_edges.reshape(shape), odd_edges.reshape(shape)
    halo = jnp.stack(
        [jnp.where(from_even, even_edges, odd_edges), jnp.where(from_even, odd_edges, even_edges)], 1
    ).reshape(ROWS * 16, LANES)
    far_halo = on_chip(swapped(halo, "lat", 1, False))
    near_block = lax.dynamic_update_slice(near_block, halo, (BLOCK, 0))
    near = on_chip(swapped(near_block, "lat", 0, False))
    inner = pl.pallas_call(
        inner_kernel,
        out_shape=chip(RANK * PLANES, LANES),
        in_specs=[VMEM] * 3,
        out_specs=VMEM,
        scratch_shapes=[
            pltpu.VMEM((2, 3, 3 * ROWS, 8, LANES), jnp.float32),
            pltpu.VMEM((3 * ROWS, 8, LANES), jnp.float32),
        ],
        name="inner", compiler_params=SMALL_VMEM,
    )(block, near, far)
    split, mean, gram = pl.pallas_call(
        side_kernel,
        out_shape=(
            pltpu.VMEM((3 * RANK, PLANES * LANES), jnp.bfloat16),
            chip(PLANES, LANES),
            chip(8, LANES),
        ),
        in_specs=[VMEM] * 7,
        out_specs=(VMEM,) * 3,
        scratch_shapes=[
            pltpu.VMEM((3, 3, 3 * ROWS, 8, LANES), jnp.float32),
            pltpu.VMEM((3, 3 * ROWS, 8, LANES), jnp.float32),
            pltpu.VMEM((RANK, ROWS * LANES), jnp.float32),
            pltpu.VMEM((RANK + 8, ROWS * LANES), jnp.float32),
        ],
        name="side", compiler_params=SMALL_VMEM,
    )(block, near, far, on_chip(halo), far_halo, on_chip(inner), on_chip(weights))
    gram = jnp.sum(sum_over(gram, "lat"), 0)
    parts = sum_over(gram, "lon")
    update, analysis = pl.pallas_call(
        analysis_kernel,
        out_shape=(f32(PLANES, LANES), f32(RANK * PLANES, LANES)),
        in_specs=[VMEM] * 3,
        out_specs=(VMEM, VMEM),
        name="analysis", compiler_params=SMALL_VMEM,
    )(on_chip(parts), on_chip(split), on_chip(mean))
    return update.reshape(background_expectation.shape), analysis.reshape(factor.shape)


def solution(mesh):
    return jax.shard_map(
        per_device,
        mesh=mesh,
        in_specs=(
            P(None, "lat", "lon"),
            P(None, None, "lat", "lon"),
            P("lat", "lon"),
            P(("lat", "lon")),
            P(("lat", "lon")),
            P(("lat", "lon")),
            P(("lat", "lon")),
        ),
        out_specs=(P(None, "lat", "lon"), P(None, None, "lat", "lon")),
        check_vma=False,
    )
```

```python
import jax
import jax.numpy as jnp
from jax import lax
from jax.experimental import pallas as pl
from jax.experimental.pallas import tpu as pltpu
from jax.sharding import PartitionSpec as P


STEPS = 4
TIME_STEP = 0.9
ROTATION = 0.25

RANK = 32
ROWS = 8
LANES = 128
HALO = 2 * STEPS
TILES = RANK // 8
PLANES = 3 * ROWS
GROUP = LANES // TILES
MAIN, SMALL, SIDE = 0, 12, 13
PER_ROW = 17
BLOCK = ROWS * PER_ROW * 8
MOVES = (0, 16, 8, 24)
PULL = 0.5 * TIME_STEP
WIDTH = 8
HIGHEST = lax.Precision.HIGHEST
NT = (((1,), (1,)), ((), ()))


def lane_iota():
    return lax.broadcasted_iota(jnp.int32, (8, LANES), 1)


def member_rows(field, row, tile):
    return pl.ds(8 * tile * PLANES + field * ROWS + row, 8, stride=PLANES)


def block_at(row, tile):
    return pl.ds((row * PER_ROW + tile) * 8, 8)


def weight_kernel(count_ref, cells_ref, values_ref, error_ref, out_ref):
    slots = cells_ref.shape[1]
    live = lax.broadcasted_iota(jnp.int32, (1, slots), 1) < count_ref[...]
    weight = jnp.where(live, 1.0, 0.0) / error_ref[...]
    square = weight * weight
    cells = cells_ref[...]
    row_of = cells // LANES
    lane_of = cells - row_of * LANES
    in_row = lax.broadcasted_iota(jnp.int32, (ROWS, slots), 0) == row_of
    spread = jnp.concatenate(
        [jnp.where(in_row, square, 0.0), jnp.where(in_row, square * values_ref[...], 0.0)], 0
    )
    in_lane = lax.broadcasted_iota(jnp.int32, (LANES, slots), 0) == lane_of
    out_ref[...] = lax.dot_general(
        spread, jnp.where(in_lane, 1.0, 0.0), NT, precision=HIGHEST, preferred_element_type=jnp.float32
    )


def pack_kernel(
    factor_ref, mean_ref, depth_ref, cells_ref, values_ref, error_ref,
    block_ref, even_edge_ref, odd_edge_ref, cells_out_ref, values_out_ref, error_out_ref,
):
    lane = lane_iota()
    part = lane // GROUP
    octet = (lane // 8) & 3
    cells_out_ref[...] = cells_ref[...]
    values_out_ref[...] = values_ref[...]
    error_out_ref[...] = error_ref[...]
    even = lax.rem(lax.axis_index("lon"), 2) == 0
    eastward, westward = {}, {}
    for row in range(ROWS):
        small = jnp.concatenate(
            [mean_ref[f * ROWS + row : f * ROWS + row + 1, :] for f in range(3)]
            + [depth_ref[row : row + 1, :]] * 5,
            0,
        )
        block_ref[block_at(row, SMALL), :] = small
        sides = []
        for field in range(3):
            side = None
            for tile in range(TILES):
                value = factor_ref[member_rows(field, row, tile), :]
                block_ref[block_at(row, MAIN + TILES * field + tile), :] = value
                moved = pltpu.roll(value, 16 + GROUP * tile, 1)
                side = moved if side is None else jnp.where(part == tile, moved, side)
            sides.append(side)
        side = pltpu.roll(small, 16, 1)
        side = jnp.where(part == 0, side, pltpu.roll(side, GROUP, 1))
        sides.append(jnp.where(part < 2, side, pltpu.roll(side, 2 * GROUP, 1)))
        for which, side in enumerate(sides):
            block_ref[block_at(row, SIDE + which), :] = side
            move = MOVES[row % 4]
            moved = pltpu.roll(side, move, 1) if move else side
            if row % 4 == 0:
                eastward[which] = westward[which] = moved
                continue
            eastward[which] = jnp.where(octet == (1 + move // 8) % 4, moved, eastward[which])
            westward[which] = jnp.where(octet == (2 + move // 8) % 4, moved, westward[which])
            if row % 4 == 3:
                at = pl.ds(((row // 4) * 4 + which) * 8, 8)
                even_edge_ref[at, :] = jnp.where(even, eastward[which], westward[which])
                odd_edge_ref[at, :] = jnp.where(even, westward[which], eastward[which])


def pulls():
    band = lax.axis_index("lat")
    bands = lax.axis_size("lat")
    north = jnp.where(band > 0, PULL, 0.0)
    south = jnp.where(band < bands - 1, PULL, 0.0)
    return north, south


def by_side(near, far):
    odd = lax.rem(lax.axis_index("lat"), 2) == 1
    return jnp.where(odd, near, far), jnp.where(odd, far, near)


def lon_difference(value):
    return pltpu.roll(value, LANES - 1, 1) - pltpu.roll(value, 1, 1)


def advance(states, row_pulls):
    north_pull, south_pull = row_pulls
    for step in range(STEPS):
        first, last = 1 + 2 * step, 3 * ROWS - 2 - 2 * step
        for state, depth in states:
            h, e, n = (state.at[field] for field in range(3))
            for row in range(first, last + 1):
                divergence = lon_difference(e[row]) + (n[row + 1] - n[row - 1])
                h[row] = h[row] - depth[row] * divergence
        for state, depth in states:
            h, e, n = (state.at[field] for field in range(3))
            for row in range(first + 1, last):
                row_pull = north_pull if row < ROWS else south_pull if row >= 2 * ROWS else PULL
                east, north = e[row], n[row]
                e[row] = east - PULL * lon_difference(h[row]) + ROTATION * north
                n[row] = north - row_pull * (h[row + 1] - h[row - 1]) - ROTATION * east


def inner_kernel(own_ref, near_ref, far_ref, out_ref, state, depth):
    def around(at):
        north, south = by_side(near_ref[at, :], far_ref[at, :])
        return enumerate((north, own_ref[at, :], south))

    for row in range(ROWS):
        for block, value in around(pl.ds((row * PER_ROW + SMALL) * 8 + 3, 1)):
            depth[ROWS * block + row] = PULL * jnp.broadcast_to(value, (8, LANES))
    row_pulls = pulls()

    def pair(which, carry):
        for half in range(2):
            tile = 2 * which + half
            for field in range(3):
                for row in range(ROWS):
                    at = pl.multiple_of((row * PER_ROW + MAIN + TILES * field + tile) * 8, 8)
                    for block, value in around(pl.ds(at, 8)):
                        state[half, field, ROWS * block + row] = value
        advance([(state.at[half], depth) for half in range(2)], row_pulls)
        for half in range(2):
            tile = 2 * which + half
            for field in range(3):
                for row in range(ROWS):
                    at = pl.multiple_of(((field * ROWS + row) * TILES + tile) * 8, 8)
                    out_ref[pl.ds(at, 8), :] = state[half, field, ROWS + row]
        return carry

    lax.fori_loop(0, TILES // 2, pair, 0)


def side_kernel(
    own_ref, near_ref, far_ref, halo_ref, near_halo_ref, far_halo_ref, inner_ref, weight_ref,
    split_ref, mean_out_ref, gram_ref, state, depth, heights, scaled,
):
    lane = lane_iota()
    low_lanes = (lane & 16) == 0
    sub = lax.broadcasted_iota(jnp.int32, (8, LANES), 0)

    def around(own, near, far, at):
        north, south = by_side(near[at, :], far[at, :])
        return north, own[at, :], south

    for row in range(ROWS):
        smalls = around(own_ref, near_ref, far_ref, block_at(row, SMALL))
        for which in range(4):
            sides = around(own_ref, near_ref, far_ref, block_at(row, SIDE + which))
            halos = around(halo_ref, near_halo_ref, far_halo_ref, pl.ds(((row // 2) * 4 + which) * 8, 8))
            for block, (small, side, halo) in enumerate(zip(smalls, sides, halos)):
                at = ROWS * block + row
                if MOVES[row % 4]:
                    halo = pltpu.roll(halo, LANES - MOVES[row % 4], 1)
                right = jnp.where(low_lanes, side, halo)
                left = jnp.where(low_lanes, halo, side)
                if which < 3:
                    state[0, which, at] = right
                    state[1, which, at] = left
                    continue
                for field in range(3):
                    state[2, field, at] = jnp.where(
                        sub == 0,
                        jnp.broadcast_to(small[field : field + 1, :], (8, LANES)),
                        jnp.where(
                            sub == 1,
                            jnp.broadcast_to(right[field : field + 1, :], (8, LANES)),
                            jnp.broadcast_to(left[field : field + 1, :], (8, LANES)),
                        ),
                    )
                of_right = PULL * jnp.broadcast_to(right[3:4, :], (8, LANES))
                of_left = PULL * jnp.broadcast_to(left[3:4, :], (8, LANES))
                whole = PULL * jnp.broadcast_to(small[3:4, :], (8, LANES))
                depth[0, at] = of_right
                depth[1, at] = of_left
                depth[2, at] = jnp.where(sub == 0, whole, jnp.where(sub == 1, of_right, of_left))
    advance([(state.at[which], depth.at[which]) for which in range(3)], pulls())

    from_right = (lane & 16) == 0
    edge = (lane < HALO) | (lane >= LANES - HALO)
    for field in range(3):
        for row in range(ROWS):
            plane = field * ROWS + row
            cols = slice(plane * LANES, (plane + 1) * LANES)
            sides = jnp.where(from_right, state[0, field, ROWS + row], state[1, field, ROWS + row])
            full = jnp.concatenate(
                [
                    jnp.where(
                        edge,
                        pltpu.roll(sides, (LANES - 16 - GROUP * tile) % LANES, 1),
                        inner_ref[pl.ds((plane * TILES + tile) * 8, 8), :],
                    )
                    for tile in range(TILES)
                ],
                0,
            )
            high = full.astype(jnp.bfloat16)
            rest = full - high.astype(jnp.float32)
            middle = rest.astype(jnp.bfloat16)
            split_ref[0:RANK, cols] = high
            split_ref[RANK : 2 * RANK, cols] = middle
            split_ref[2 * RANK : 3 * RANK, cols] = (rest - middle.astype(jnp.float32)).astype(jnp.bfloat16)
            mine = state[2, field, ROWS + row]
            both = jnp.where(from_right[0:1], mine[1:2, :], mine[2:3, :])
            mean = jnp.where(edge[0:1], pltpu.roll(both, LANES - 16, 1), mine[0:1, :])
            mean_out_ref[plane : plane + 1, :] = mean
            if field == 0:
                square = weight_ref[row : row + 1, :]
                heights[:, cols] = full
                scaled[0:RANK, cols] = full * square
                pulled = weight_ref[ROWS + row : ROWS + row + 1, :] - square * mean
                scaled[RANK : RANK + 8, cols] = jnp.broadcast_to(pulled, (8, LANES))
    gram = lax.dot_general(
        heights[...], scaled[...], NT, precision=HIGHEST, preferred_element_type=jnp.float32
    )
    gram = jnp.concatenate([gram, jnp.zeros((RANK, LANES - RANK - 8), jnp.float32)], 1)
    acc = None
    for tile in range(TILES):
        part = gram[8 * tile : 8 * tile + 8, :]
        if tile < 2:
            far = gram[8 * tile + 16 : 8 * tile + 24, :]
            part = jnp.where(lane == 31, pltpu.roll(part, LANES - 1, 1), part)
            part = jnp.where(lane == 30, pltpu.roll(far, LANES - 2, 1), part)
        moved = pltpu.roll(part, 32 * tile, 1) if tile else part
        acc = moved if acc is None else jnp.where(lane // 32 == tile, moved, acc)
    gram_ref[...] = acc


def analysis_kernel(parts_ref, split_ref, mean_ref, update_ref, factor_ref):
    lane = lane_iota()
    total = jnp.sum(parts_ref[...], 0)
    tiles, drives = [], [None] * TILES
    for tile in range(TILES):
        part = pltpu.roll(total, LANES - 32 * tile, 1) if tile else total
        if tile < 2:
            drives[tile] = pltpu.roll(part, 2 * RANK - 31, 1)
            drives[tile + 2] = pltpu.roll(part, 2 * RANK - 30, 1)
        tiles.append(part)
    lower = jnp.concatenate(tiles, 0)
    wide = lax.broadcasted_iota(jnp.int32, (RANK, LANES), 1)
    deep = lax.broadcasted_iota(jnp.int32, (RANK, LANES), 0)
    mirrored = jnp.concatenate([lower, jnp.zeros((LANES - RANK, LANES), jnp.float32)], 0).T[0:RANK, :]
    work = jnp.where(wide > deep, mirrored, lower)
    work = jnp.where(wide < RANK, work, 0.0) + jnp.where((wide == deep) | (wide == deep + RANK), 1.0, 0.0)
    work = jnp.where(wide == 2 * RANK, jnp.concatenate(drives, 0), work)
    for first in range(0, RANK, WIDTH):
        columns = [jnp.broadcast_to(work[:, k : k + 1], (RANK, LANES)) for k in range(first, first + WIDTH)]
        rows = [work[k : k + 1, :] for k in range(first, first + WIDTH)]
        for j in range(WIDTH):
            k = first + j
            inverse = 1.0 / columns[j][k : k + 1, :]
            scaled_row = rows[j] * inverse
            for i in range(j + 1, WIDTH):
                ratio = columns[j][first + i : first + i + 1, :] * inverse
                rows[i] = rows[i] - ratio * rows[j]
                columns[i] = columns[i] - columns[j] * ratio
            work = work - jnp.where(deep > k, columns[j], 0.0) * scaled_row
    pivots = jnp.sum(jnp.where(wide == deep, work, 0.0), 1, keepdims=True)
    work = work * lax.rsqrt(pivots)
    shift = jnp.sum(work * work[:, 2 * RANK : 2 * RANK + 1], 0, keepdims=True)
    mixed = jnp.concatenate([work, jnp.broadcast_to(shift, (8, LANES))], 0)[:, RANK : 2 * RANK]
    high = mixed.astype(jnp.bfloat16)
    rest = mixed - high.astype(jnp.float32)
    middle = rest.astype(jnp.bfloat16)
    low = (rest - middle.astype(jnp.float32)).astype(jnp.bfloat16)
    left = jnp.concatenate([high, high, high, middle, middle, low], 1)
    split = split_ref[...]
    fine = jnp.concatenate([split, split[0 : 2 * RANK], split[0:RANK]], 0)
    out = jnp.dot(left, fine, preferred_element_type=jnp.float32)
    for plane in range(PLANES):
        cols = slice(plane * LANES, (plane + 1) * LANES)
        for tile in range(TILES):
            factor_ref[pl.ds(8 * tile * PLANES + plane, 8, stride=PLANES), :] = out[8 * tile : 8 * tile + 8, cols]
        update_ref[plane : plane + 1, :] = mean_ref[plane : plane + 1, :] + out[RANK : RANK + 1, cols]


VMEM = pl.BlockSpec(memory_space=pltpu.VMEM)
SMALL_VMEM = pltpu.CompilerParams(vmem_limit_bytes=8 << 20)


def f32(*shape):
    return jax.ShapeDtypeStruct(shape, jnp.float32)


def chip(*shape):
    return pltpu.VMEM(shape, jnp.float32)


def on_chip(value):
    return pltpu.with_memory_space_constraint(value, pltpu.VMEM)


def swapped(value, axis, offset, periodic):
    count = lax.axis_size(axis)
    pairs = [(i, i + 1) for i in range(offset, count - 1, 2)]
    if offset and periodic:
        pairs.append((count - 1, 0))
    return lax.ppermute(value, axis, pairs + [(j, i) for i, j in pairs])


def sum_over(value, axis):
    count = lax.axis_size(axis)
    sent = jnp.broadcast_to(value[None], (count, *value.shape))
    return lax.all_to_all(sent, axis, 0, 0)


def per_device(
    background_expectation, factor, average_thickness, obs_cells, obs_count, obs_values, obs_error
):
    assert factor.shape == (RANK, 3, ROWS, LANES)
    slots = obs_cells.shape[0]
    block, even_edges, odd_edges, cells, values, error = pl.pallas_call(
        pack_kernel,
        out_shape=(
            chip(BLOCK, LANES),
            chip(ROWS * 8, LANES),
            chip(ROWS * 8, LANES),
            pltpu.VMEM((1, slots), jnp.int32),
            chip(1, slots),
            chip(1, slots),
        ),
        in_specs=[VMEM] * 6,
        out_specs=(VMEM,) * 6,
        name="pack",
    )(
        factor.reshape(RANK * PLANES, LANES), background_expectation.reshape(PLANES, LANES), average_thickness,
        obs_cells.reshape(1, slots), obs_values.reshape(1, slots), obs_error.reshape(1, slots),
    )
    block = on_chip(block)
    odd_edges = swapped(odd_edges, "lon", 1, True)
    far = on_chip(swapped(block, "lat", 1, False))
    even_edges = swapped(even_edges, "lon", 0, True)
    near = on_chip(swapped(block, "lat", 0, False))
    weights = pl.pallas_call(
        weight_kernel, out_shape=chip(2 * ROWS, LANES), in_specs=[VMEM] * 4, out_specs=VMEM, name="weigh"
    )(obs_count.reshape(1, 1), on_chip(cells), on_chip(values), on_chip(error))
    shape = (ROWS // 4, 4 * 8, LANES)
    eastern = (lax.broadcasted_iota(jnp.int32, shape, 2) & 8) // 8 != 1
    from_even = eastern == (lax.rem(lax.axis_index("lon"), 2) == 0)
    even_edges, odd_edges = even_edges.reshape(shape), odd_edges.reshape(shape)
    halo = jnp.stack(
        [jnp.where(from_even, even_edges, odd_edges), jnp.where(from_even, odd_edges, even_edges)], 1
    ).reshape(ROWS * 16, LANES)
    far_halo = on_chip(swapped(halo, "lat", 1, False))
    near_halo = on_chip(swapped(halo, "lat", 0, False))
    inner = pl.pallas_call(
        inner_kernel,
        out_shape=chip(RANK * PLANES, LANES),
        in_specs=[VMEM] * 3,
        out_specs=VMEM,
        scratch_shapes=[
            pltpu.VMEM((2, 3, 3 * ROWS, 8, LANES), jnp.float32),
            pltpu.VMEM((3 * ROWS, 8, LANES), jnp.float32),
        ],
        name="inner", compiler_params=SMALL_VMEM,
    )(block, near, far)
    split, mean, gram = pl.pallas_call(
        side_kernel,
        out_shape=(
            pltpu.VMEM((3 * RANK, PLANES * LANES), jnp.bfloat16),
            chip(PLANES, LANES),
            chip(8, LANES),
        ),
        in_specs=[VMEM] * 8,
        out_specs=(VMEM,) * 3,
        scratch_shapes=[
            pltpu.VMEM((3, 3, 3 * ROWS, 8, LANES), jnp.float32),
            pltpu.VMEM((3, 3 * ROWS, 8, LANES), jnp.float32),
            pltpu.VMEM((RANK, ROWS * LANES), jnp.float32),
            pltpu.VMEM((RANK + 8, ROWS * LANES), jnp.float32),
        ],
        name="side", compiler_params=SMALL_VMEM,
    )(block, near, far, on_chip(halo), near_halo, far_halo, on_chip(inner), on_chip(weights))
    gram = jnp.sum(sum_over(gram, "lat"), 0)
    parts = sum_over(gram, "lon")
    update, analysis = pl.pallas_call(
        analysis_kernel,
        out_shape=(f32(PLANES, LANES), f32(RANK * PLANES, LANES)),
        in_specs=[VMEM] * 3,
        out_specs=(VMEM, VMEM),
        name="analysis", compiler_params=SMALL_VMEM,
    )(on_chip(parts), on_chip(split), on_chip(mean))
    return update.reshape(background_expectation.shape), analysis.reshape(factor.shape)


def solution(mesh):
    return jax.shard_map(
        per_device,
        mesh=mesh,
        in_specs=(
            P(None, "lat", "lon"),
            P(None, None, "lat", "lon"),
            P("lat", "lon"),
            P(("lat", "lon")),
            P(("lat", "lon")),
            P(("lat", "lon")),
            P(("lat", "lon")),
        ),
        out_specs=(P(None, "lat", "lon"), P(None, None, "lat", "lon")),
        check_vma=False,
    )
```
